32 devices in a mesh: pole: 2 (over y), row: 4 (over z), col: 4 (over x, core).
Axes of the slice: x: 2, y: 2, z: 4, core: 2. Of those that a mesh axis runs over, the one named last changes fastest.
Arguments:
- root_inverse: float32 [16384, 8192], P(('pole', 'row'), 'col'), parts along dimension 0, may hold values from -6 to 6
- lower_one: float32 [16384, 512], P(('pole', 'row'), 'col'), parts along dimension 0, may hold values from -0.0625 to 0.0625
- pattern_one: int32 [64, 4], replicated, may hold values from 0 to 1, as said below
- diag_one: float32 [256, 512], P('pole', 'col'), parts along dimension 0, may hold values from -6 to 6
- lower_two: float32 [16384, 1024], P(('pole', 'row'), 'col'), parts along dimension 0, may hold values from -0.0625 to 0.0625
- pattern_two: int32 [64, 8], replicated, may hold values from 0 to 1, as said below
- parent_two: int32 [8], replicated, may hold values from 0 to 3, as said below
- lower_parent: float32 [256, 1024], P('pole', 'col'), parts along dimension 0, may hold values from -0.5 to 0.5
- diag_two: float32 [256, 1024], P('pole', 'col'), parts along dimension 0, may hold values from -6 to 6
Outputs:
- inverse_off_one: float32 [16384, 512], P(('pole', 'row'), 'col'), parts along dimension 0
- inverse_diagonal_first: float32 [256, 512], P('pole', 'col'), parts along dimension 0
- inverse_off_two: float32 [16384, 1024], P(('pole', 'row'), 'col'), parts along dimension 0
- inverse_parent_two: float32 [256, 1024], P('pole', 'col'), parts along dimension 0
- inverse_diag_two: float32 [256, 1024], P('pole', 'col'), parts along dimension 0
The draws below stay inside these ranges and needn't reach their ends.
There are 2 independent parts, one for each index of `pole`. The reference program is written for one: setup_inputs(seed, part) draws one part's arguments, and reference() takes and returns one part's arrays. A program takes and returns all parts, laid end to end along the dimension named above; an argument that names none is the same for every part. Nothing has to cross between parts.
Inputs may be any that keep to these rules, and one draw needn't show every extreme that they name: pattern_one[i, k] is 1 where root block row i lies in the structure of first-level supernode k. `parent_two`: each first-level supernode is the parent of exactly two second-level supernodes. pattern_two[i, m] is 1 only where pattern_one[i, parent_two[m]] is 1.
All inputs are finite; a program needn't handle non-finite values.
Results may differ from the reference program's by a relative error of at most 0.000088.
Values sent between devices are 32-bit elements; how exact they have to be, the bound alone decides.
No kernel may reach another device: no remote copies, remote signals or barrier semaphores. Data moves between devices by JAX's collectives and lax.ppermute only.
A program may use at most 128 MiB of HBM per device.

```python
import jax
import jax.numpy as jnp
from jax import lax

BLOCK_SIDE = 128
ROOT_BLOCKS = 64
SUPERNODES_FIRST = 4
SUPER_TWO = 8
ROOT_ORDER = 8192
ORDER_ONE = 512
ORDER_TWO = 1024


def structure(key):
    level_key = jax.random.fold_in(key, 101)
    entry_key = jax.random.fold_in(key, 202)
    parent_key = jax.random.fold_in(key, 303)
    retain_key = jax.random.fold_in(key, 404)
    density = jax.random.randint(level_key, (ROOT_BLOCKS, 1), 0, 8)
    first = (jax.random.randint(entry_key, (ROOT_BLOCKS, SUPERNODES_FIRST), 0, 8) < density).astype(jnp.int32)
    pair_ids = jnp.arange(SUPERNODES_FIRST, dtype=jnp.int32)
    far_parent = (pair_ids + SUPERNODES_FIRST // 2) % SUPERNODES_FIRST
    drawn_parent = jax.random.permutation(parent_key, pair_ids).astype(jnp.int32)
    parents = jnp.stack([far_parent, drawn_parent], axis=1).reshape(SUPER_TWO).astype(jnp.int32)
    retained = jax.random.randint(retain_key, (ROOT_BLOCKS, SUPER_TWO), 0, 4) < 3
    second = jnp.where(retained, first[:, parents], 0).astype(jnp.int32)
    return (first, parents, second)


def draw_pattern_one(key, part):
    return structure(key)[0]


def draw_parent_two(key, part):
    return structure(key)[1]


def draw_pattern_two(key, part):
    return structure(key)[2]


def levels(own_key, shape, shards, low, high):
    factor_of = 1.0
    for position, parts in shards:
        heights = jax.random.uniform(jax.random.fold_in(jax.random.fold_in(own_key, 6), position), (parts,), jnp.float32, low / len(shards), high / len(shards))
        factor_of = factor_of * jnp.repeat(jnp.exp(heights), shape[position] // parts).reshape((-1,) + (1,) * (len(shape) - 1 - position))
    return factor_of


def bell_draw(key, shape, scale, bound, pieces=(), kind=jnp.bfloat16):
    factor_of = levels(key, shape, pieces, -0.22, 0.18) if pieces else 1.0
    values = jax.random.normal(key, shape, jnp.float32) * scale * factor_of
    return jnp.minimum(jnp.maximum(values, -bound), bound).astype(kind)


def setup_inputs(seed: int = 0, part: int = 0) -> dict:
    streams_of = jax.random.split(jax.random.key(seed), 10)
    part_keys = jax.random.split(jax.random.fold_in(streams_of[9], part), 10)
    root_inverse = bell_draw(part_keys[0], (ROOT_ORDER, ROOT_ORDER), 1.0, 6.0, ((0, 4), (1, 4)), jnp.float32)
    lower_one = bell_draw(part_keys[1], (ROOT_ORDER, ORDER_ONE), ROOT_ORDER ** -0.5, 0.0625, ((0, 4), (1, 4)), jnp.float32)
    pattern_one = draw_pattern_one(jax.random.fold_in(streams_of[9], 71), part)
    diag_one = bell_draw(part_keys[3], (BLOCK_SIDE, ORDER_ONE), 1.0, 6.0, ((1, 4),), jnp.float32)
    lower_two = bell_draw(part_keys[4], (ROOT_ORDER, ORDER_TWO), ROOT_ORDER ** -0.5, 0.0625, ((0, 4), (1, 4)), jnp.float32)
    pattern_two = draw_pattern_two(jax.random.fold_in(streams_of[9], 71), part)
    parent_two = draw_parent_two(jax.random.fold_in(streams_of[9], 71), part)
    lower_parent = bell_draw(part_keys[7], (BLOCK_SIDE, ORDER_TWO), BLOCK_SIDE ** -0.5, 0.5, ((1, 4),), jnp.float32)
    diag_two = bell_draw(part_keys[8], (BLOCK_SIDE, ORDER_TWO), 1.0, 6.0, ((1, 4),), jnp.float32)
    return dict(root_inverse=root_inverse, lower_one=lower_one, pattern_one=pattern_one, diag_one=diag_one, lower_two=lower_two, pattern_two=pattern_two, parent_two=parent_two, lower_parent=lower_parent, diag_two=diag_two)


PRECISION_MODE = lax.Precision.HIGHEST


def expand_blocks(pattern):
    count_rows, count_cols = pattern.shape
    spread = jnp.broadcast_to(pattern.astype(jnp.float32)[:, None, :, None], (count_rows, BLOCK_SIDE, count_cols, BLOCK_SIDE))
    return spread.reshape(count_rows * BLOCK_SIDE, count_cols * BLOCK_SIDE)


def block_inner(masked, solved):
    rows_here = masked.shape[0]
    blocks = masked.shape[1] // BLOCK_SIDE
    inner = jnp.einsum("ikb,ikc->bkc", masked.reshape(rows_here, blocks, BLOCK_SIDE), solved.reshape(rows_here, blocks, BLOCK_SIDE), precision=PRECISION_MODE)
    return inner.reshape(BLOCK_SIDE, blocks * BLOCK_SIDE)


def reference(root_inverse, lower_one, pattern_one, diag_one, lower_two, pattern_two, parent_two, lower_parent, diag_two):
    mask_one = expand_blocks(pattern_one)
    masked_one = lower_one * mask_one
    solved_one = jnp.dot(root_inverse, masked_one, precision=PRECISION_MODE, preferred_element_type=jnp.float32)
    inverse_off_one = -(mask_one * solved_one)
    inverse_diagonal_first = diag_one + block_inner(masked_one, solved_one)
    mask_two = expand_blocks(pattern_two)
    masked_two = lower_two * mask_two
    selection_matrix = (parent_two[None, :] == jnp.arange(SUPERNODES_FIRST, dtype=jnp.int32)[:, None]).astype(jnp.float32)
    parent_cols = jnp.einsum("ikb,km->imb", inverse_off_one.reshape(ROOT_ORDER, SUPERNODES_FIRST, BLOCK_SIDE), selection_matrix, precision=PRECISION_MODE)
    link = lower_parent.reshape(BLOCK_SIDE, SUPER_TWO, BLOCK_SIDE)
    solved_two = jnp.dot(root_inverse, masked_two, precision=PRECISION_MODE, preferred_element_type=jnp.float32)
    solved_two = solved_two + jnp.einsum("imb,bme->ime", parent_cols, link, precision=PRECISION_MODE).reshape(ROOT_ORDER, ORDER_TWO)
    parent_diagonal = jnp.einsum("vfl,fo->vol", inverse_diagonal_first.reshape(BLOCK_SIDE, SUPERNODES_FIRST, BLOCK_SIDE), selection_matrix, precision=PRECISION_MODE)
    across = jnp.einsum("imb,ime->bme", parent_cols, masked_two.reshape(ROOT_ORDER, SUPER_TWO, BLOCK_SIDE), precision=PRECISION_MODE)
    across = across + jnp.einsum("bmd,dme->bme", parent_diagonal, link, precision=PRECISION_MODE)
    inverse_diag_two = diag_two + block_inner(masked_two, solved_two)
    inverse_diag_two = inverse_diag_two + jnp.einsum("dmb,dme->bme", link, across, precision=PRECISION_MODE).reshape(BLOCK_SIDE, ORDER_TWO)
    return (inverse_off_one, inverse_diagonal_first, -(mask_two * solved_two), -across.reshape(BLOCK_SIDE, ORDER_TWO), inverse_diag_two)
```

```python
import functools

import jax
import jax.numpy as jnp
from jax import lax
from jax.experimental import pallas as pl
from jax.experimental.pallas import tpu as pltpu
from jax.sharding import PartitionSpec as P

SIDE = 128
PAIR = 2 * SIDE
GROUP_ROWS = 2
GROUP_COLS = 4
EXACT = lax.Precision.HIGHEST
VMEM_BYTES = 56 * 1024 * 1024
ROOT_COPIES = 8

SMEM_SPEC = pl.BlockSpec(memory_space=pltpu.SMEM)
VMEM_SPEC = pl.BlockSpec(memory_space=pltpu.VMEM)
ANY_SPEC = pl.BlockSpec(memory_space=pl.ANY)


def shape_f32(rows, cols):
    return jax.ShapeDtypeStruct((rows, cols), jnp.float32)


def call(body, outs, smem, vmem, scratch=(), far=()):
    return pl.pallas_call(
        body,
        out_shape=outs,
        in_specs=[SMEM_SPEC] * len(smem) + [ANY_SPEC] * len(far) + [VMEM_SPEC] * len(vmem),
        out_specs=jax.tree.map(lambda _: VMEM_SPEC, outs),
        scratch_shapes=list(scratch),
        compiler_params=pltpu.CompilerParams(vmem_limit_bytes=VMEM_BYTES),
    )(*smem, *far, *vmem)


def halves(value):
    high = value.astype(jnp.bfloat16)
    low = (value - high.astype(jnp.float32)).astype(jnp.bfloat16)
    return high, low


def beside(value):
    return jnp.concatenate(halves(value), axis=1)


def above(value):
    return jnp.concatenate(halves(value), axis=0)


def fold_cols(value):
    return value[:, :SIDE] + value[:, SIDE:]


def fold_all(value):
    rows = value.shape[0] // 2
    return fold_cols(value[:rows] + value[rows:])


def inner(left, right):
    return fold_all(
        lax.dot_general(
            beside(left),
            beside(right),
            (((0,), (0,)), ((), ())),
            preferred_element_type=jnp.float32,
        )
    )


def block_at(index):
    return pl.ds(pl.multiple_of(index * SIDE, SIDE), SIDE)


def rounded(count, step):
    return -(-count // step) * step


def pack_body(row_blocks, where_ref, pattern, source, target):
    row_start = where_ref[0] * row_blocks
    col_index = where_ref[1]
    filled = jnp.int32(0)
    owned = source.shape[1] // SIDE
    for local in range(owned):

        def step(block, count, local=local):
            active = pattern[row_start + block, col_index * owned + local] > 0

            @pl.when(active)
            def _():
                target[block_at(count), :] = source[block_at(block), local * SIDE : (local + 1) * SIDE]

            return count + active.astype(jnp.int32)

        filled = lax.fori_loop(0, row_blocks, step, filled)


def pack(where, pattern, source, capacity):
    return call(
        functools.partial(pack_body, source.shape[0] // SIDE),
        shape_f32(capacity * SIDE, SIDE),
        [where, pattern],
        [source],
    )


def split_body(source, target):
    cols = source.shape[1]
    high, low = halves(source[...])
    target[:, :cols] = high
    target[:, cols:] = low


def split_root(root):
    rows, cols = root.shape
    step = min(rows, 256)
    return pl.pallas_call(
        split_body,
        out_shape=jax.ShapeDtypeStruct((rows, 2 * cols), jnp.bfloat16),
        grid=(rows // step,),
        in_specs=[pl.BlockSpec((step, cols), lambda i: (i, 0))],
        out_specs=pl.BlockSpec((step, 2 * cols), lambda i: (i, 0)),
        compiler_params=pltpu.CompilerParams(vmem_limit_bytes=VMEM_BYTES),
    )(root)


def line_body(ranks_col, piece_rows, where_ref, bases, *refs):
    parts, rest = refs[:ranks_col], refs[ranks_col:]
    outs, line = rest[:ranks_col], rest[ranks_col]
    col_index = where_ref[1]
    for hop in range(ranks_col):
        owner = col_index ^ hop
        base = bases[owner]

        def step(slot, carry, hop=hop, base=base):
            line[block_at(base + slot), :] = parts[hop][block_at(slot), :]
            return carry

        lax.fori_loop(0, bases[owner + 1] - base, step, jnp.int32(0))
    for step in range(ranks_col):
        at = ((col_index ^ step) * ranks_col + step) * piece_rows
        outs[step][...] = line[pl.ds(pl.multiple_of(at, 8), piece_rows), :]


class Plan:
    def __init__(self, rows, cols):
        self.rows = rounded(rows, GROUP_COLS)
        self.cols = rounded(cols, GROUP_COLS)
        self.row_block = 2
        self.row_slot = self.row_block + self.rows
        self.row_first = self.row_slot + self.rows
        self.col_block = self.row_first + self.rows
        self.col_slot = self.col_block + self.cols
        self.stride = self.col_slot + self.cols


def listed(active, values, length):
    blocks = active.shape[0]
    before = (jnp.arange(blocks)[None, :] < jnp.arange(blocks)[:, None]).astype(jnp.int32)
    rank = jnp.sum(before[:, :, None] * active[None], axis=1)
    count = jnp.sum(active, axis=0)
    wanted = jnp.minimum(jnp.arange(length)[:, None], count[None, :] - 1)
    hit = jnp.where(rank[None] == wanted[:, None, :], active[None], 0)
    return [jnp.sum(hit * value[None], axis=1).T for value in values], count


def make_plan(active_row, slot_row, first_row, active_col, slot_col):
    plan = Plan(active_row.shape[0], active_col.shape[0])
    number = lambda active: jnp.broadcast_to(jnp.arange(active.shape[0])[:, None], active.shape)
    rows, count_rows = listed(active_row, [number(active_row), slot_row, first_row], plan.rows)
    cols, count_cols = listed(active_col, [number(active_col), slot_col], plan.cols)
    table = jnp.concatenate([count_rows[:, None], count_cols[:, None], *rows, *cols], axis=1)
    return plan, table.astype(jnp.int32).reshape(-1)


def root_body(plan, ranks_col, owned, capacity, second, where_ref, table, root_ref, gathered, *refs):
    if second:
        known, *refs = refs
        outs, refs = refs[:ranks_col], refs[ranks_col:]
    else:
        outs, everything, *refs = refs[:ranks_col], *refs[ranks_col:]
    weights, root, starts, arrived = refs
    col_index = where_ref[1]
    nodes = ranks_col * owned
    cols = root.shape[1] // 2
    share = root.shape[0] // arrived.shape[0]
    copies = [
        pltpu.make_async_copy(
            root_ref.at[pl.ds(t * share, share), :], root.at[pl.ds(t * share, share), :], arrived.at[t]
        )
        for t in range(arrived.shape[0])
    ]
    for copy in copies:
        copy.start()

    def prepare(node, base):
        starts[node] = base
        at = node * plan.stride
        count = table[at + 1]

        def fill(t, carry):
            slot = table[at + plan.col_slot + t]
            weights[block_at(base + t), :] = beside(gathered[block_at(slot), :])
            return carry

        def clear(t, carry):
            weights[block_at(base + t), :] = jnp.zeros((SIDE, PAIR), jnp.bfloat16)
            return carry

        lax.fori_loop(0, count, fill, jnp.int32(0))
        upper = (count + GROUP_COLS - 1) // GROUP_COLS * GROUP_COLS
        lax.fori_loop(count, upper, clear, jnp.int32(0))
        return base + upper

    lax.fori_loop(0, nodes, prepare, jnp.int32(0))
    for copy in copies:
        copy.wait()

    def per_node(node, carry):
        at = node * plan.stride
        base = starts[node]
        hop = (node // owned) ^ col_index
        groups = (table[at + 1] + GROUP_COLS - 1) // GROUP_COLS

        def row_group(group, carry):
            blocks = [table[at + plan.row_block + group * GROUP_ROWS + t] for t in range(GROUP_ROWS)]

            def col_group(step, total):
                columns = [
                    pl.multiple_of(table[at + plan.col_block + step * GROUP_COLS + q] * SIDE, SIDE)
                    for q in range(GROUP_COLS)
                ]
                tiles = [
                    jnp.concatenate(
                        [root[block_at(block), pl.ds(shift + column, SIDE)] for column in columns], axis=1
                    )
                    for shift in (0, cols)
                    for block in blocks
                ]
                start = pl.multiple_of((base + step * GROUP_COLS) * SIDE, GROUP_COLS * SIDE)
                made = jnp.dot(
                    jnp.concatenate(tiles, axis=0),
                    weights[pl.ds(start, GROUP_COLS * SIDE), :],
                    preferred_element_type=jnp.float32,
                )
                return total + fold_all(made)

            total = lax.fori_loop(
                0, groups, col_group, jnp.zeros((GROUP_ROWS * SIDE, SIDE), jnp.float32)
            )
            for t in range(GROUP_ROWS):
                slot = table[at + plan.row_slot + group * GROUP_ROWS + t]
                value = total[t * SIDE : (t + 1) * SIDE]
                if second:
                    value = value - known[block_at(slot), :]
                else:
                    everything[block_at(slot), :] = value
                for other in range(ranks_col):

                    @pl.when(hop == other)
                    def _(other=other, slot=slot, value=value):
                        outs[other][block_at(slot - other * capacity), :] = value

            return carry

        return lax.fori_loop(0, (table[at] + GROUP_ROWS - 1) // GROUP_ROWS, row_group, carry)

    lax.fori_loop(0, nodes, per_node, jnp.int32(0))


def root_partials(where, plan, table, root, gathered, ranks_col, owned, capacity, known=None):
    rows, wide = root.shape
    nodes = ranks_col * owned
    room = min(nodes * plan.cols, rounded(gathered.shape[0] // SIDE, GROUP_COLS) + nodes * GROUP_COLS)
    copies = ROOT_COPIES if rows % (ROOT_COPIES * 16) == 0 else 1
    outs = [shape_f32(capacity * SIDE, SIDE)] * ranks_col
    if known is None:
        outs = outs + [shape_f32(ranks_col * capacity * SIDE, SIDE)]
    return call(
        functools.partial(root_body, plan, ranks_col, owned, capacity, known is not None),
        outs,
        [where, table],
        [gathered] if known is None else [gathered, known],
        [
            pltpu.VMEM((room * SIDE, PAIR), jnp.bfloat16),
            pltpu.VMEM((rows, wide), jnp.bfloat16),
            pltpu.SMEM((nodes,), jnp.int32),
            pltpu.SemaphoreType.DMA((copies,)),
        ],
        [root],
    )


def link_body(plan, table, firsts, link, out):
    nodes = link.shape[1] // SIDE

    def per_node(node, carry):
        at = node * plan.stride
        block = beside(link[:, block_at(node)])

        def step(t, carry):
            first = table[at + plan.row_first + t]
            slot = table[at + plan.row_slot + t]
            made = jnp.dot(above(firsts[block_at(first), :]), block, preferred_element_type=jnp.float32)
            out[block_at(slot), :] = fold_all(made)
            return carry

        return lax.fori_loop(0, table[at], step, carry)

    lax.fori_loop(0, nodes, per_node, jnp.int32(0))


def first_body(row_blocks, ranks_col, where_ref, pattern, position, pattern_two, position_two, kids, *refs):
    mine, near, far, packed, *rest = refs
    blocks_two, (off, sums, total) = rest[:ranks_col], rest[ranks_col:]
    row_start = where_ref[0] * row_blocks
    col_index = where_ref[1]
    owned = off.shape[1] // SIDE
    owned_two = pattern_two.shape[1] // ranks_col
    total[...] = mine[...] + near[...] + far[...]
    sums[...] = jnp.zeros(sums.shape, jnp.float32)
    for local in range(owned):
        node = col_index * owned + local
        lanes = slice(local * SIDE, (local + 1) * SIDE)

        def step(block, carry):
            place = row_start + block
            slot = position[place, node]
            active = pattern[place, node] > 0

            @pl.when(active)
            def _():
                value = total[block_at(slot), :]
                off[block_at(block), lanes] = -value
                sums[0:SIDE, lanes] += inner(packed[block_at(slot), :], value)

            @pl.when(jnp.logical_not(active))
            def _():
                off[block_at(block), lanes] = jnp.zeros((SIDE, SIDE), jnp.float32)

            for kid in range(2):
                child = kids[2 * local + kid]
                hop = col_index ^ (child // owned_two)
                slot_two = position_two[place, child]

                @pl.when(pattern_two[place, child] > 0)
                def _(kid=kid, hop=hop, slot_two=slot_two):
                    for other in range(ranks_col):

                        @pl.when(hop == other)
                        def _(other=other):
                            sums[(1 + kid) * SIDE : (2 + kid) * SIDE, lanes] += inner(
                                total[block_at(slot), :], blocks_two[other][block_at(slot_two), :]
                            )

            return carry

        lax.fori_loop(0, row_blocks, step, jnp.int32(0))


def second_body(row_blocks, where_ref, pattern, position, mine, near, far, packed, off, sums, total):
    row_start = where_ref[0] * row_blocks
    col_index = where_ref[1]
    owned = off.shape[1] // SIDE
    total[...] = mine[...] + near[...] + far[...]
    sums[...] = jnp.zeros(sums.shape, jnp.float32)
    for local in range(owned):
        node = col_index * owned + local
        lanes = slice(local * SIDE, (local + 1) * SIDE)

        def step(block, carry):
            place = row_start + block
            slot = position[place, node]
            active = pattern[place, node] > 0

            @pl.when(active)
            def _():
                value = total[block_at(slot), :]
                off[block_at(block), lanes] = -value
                sums[:, lanes] += inner(packed[block_at(slot), :], value)

            @pl.when(jnp.logical_not(active))
            def _():
                off[block_at(block), lanes] = jnp.zeros((SIDE, SIDE), jnp.float32)

            return carry

        lax.fori_loop(0, row_blocks, step, jnp.int32(0))


def tail_body(kids, diag, sums, link, diagonal, made):
    owned = diag.shape[1] // SIDE
    for local in range(owned):
        lanes = slice(local * SIDE, (local + 1) * SIDE)
        own = diag[:, lanes] + sums[0:SIDE, lanes]
        diagonal[:, lanes] = own
        for kid in range(2):
            step = link[:, block_at(kids[2 * local + kid])]
            share = sums[(1 + kid) * SIDE : (2 + kid) * SIDE, lanes]
            across = jnp.dot(own, step, precision=EXACT, preferred_element_type=jnp.float32) - share
            at = (2 * local + kid) * SIDE
            made[at : at + SIDE, 0:SIDE] = -across
            made[at : at + SIDE, SIDE:PAIR] = inner(step, across)


def swap_col(value, hop):
    ranks = lax.axis_size("col")
    return lax.ppermute(value, "col", [(c, c ^ hop) for c in range(ranks)])


def gather_col(value):
    across = swap_col(value, 2)
    return [value, swap_col(value, 1), across, swap_col(across, 1)]


def exchange_col(value, col_index, chunk):
    piece = lambda hop: lax.dynamic_slice_in_dim(value, (col_index ^ hop) * chunk, chunk, 0)
    moved = [swap_col(piece(hop), hop) for hop in (3, 2, 1)]
    return jnp.concatenate([piece(0), moved[2], moved[1], moved[0]], axis=0)


def turn(pieces):
    ranks = len(pieces)
    return jnp.concatenate(
        [
            lax.ppermute(
                piece,
                ("row", "col"),
                [(r * ranks + c, (c ^ u) * ranks + r) for r in range(ranks) for c in range(ranks)],
            )
            for u, piece in enumerate(pieces)
        ],
        axis=0,
    )


def scatter_col(parts):
    relay = parts[2] + swap_col(parts[3], 1)
    return parts[0], swap_col(parts[1], 1), swap_col(relay, 2), relay


def sum_row(value):
    ranks = lax.axis_size("row")
    reach = 1
    while reach < ranks:
        value = value + lax.ppermute(value, "row", [(r, r ^ reach) for r in range(ranks)])
        reach *= 2
    return value


def counts(pattern, row_blocks, ranks_col):
    blocks, nodes = pattern.shape
    return jnp.sum(
        pattern.reshape(blocks // row_blocks, row_blocks, ranks_col, nodes // ranks_col), axis=(1, 3)
    )


def positions(pattern, row_blocks, ranks_col):
    blocks, nodes = pattern.shape
    owned = nodes // ranks_col
    many = owned * row_blocks
    flat = (
        pattern.reshape(blocks // row_blocks, row_blocks, ranks_col, owned)
        .transpose(0, 2, 3, 1)
        .reshape(blocks // row_blocks, ranks_col, many)
    )
    before = (jnp.arange(many)[None, :] < jnp.arange(many)[:, None]).astype(jnp.int32)
    rank = jnp.sum(flat[:, :, None, :] * before[None, None], axis=-1)
    return (
        rank.reshape(blocks // row_blocks, ranks_col, owned, row_blocks)
        .transpose(0, 3, 1, 2)
        .reshape(blocks, nodes)
        .astype(jnp.int32)
    )


def after(value, *others):
    return lax.optimization_barrier((value, *others))[0]


def sparse_plan(
    capacities,
    root_inverse,
    lower_one,
    pattern_one,
    diag_one,
    lower_two,
    pattern_two,
    parent_two,
    lower_parent,
    diag_two,
):
    capacity_one, capacity_two, capacity_line = capacities
    rows_here, cols_here = root_inverse.shape
    row_blocks = rows_here // SIDE
    col_blocks = cols_here // SIDE
    ranks_row = lax.axis_size("row")
    ranks_col = lax.axis_size("col")
    turned = ranks_row == ranks_col
    group = ranks_row // ranks_col
    row_index = lax.axis_index("row")
    col_index = lax.axis_index("col")
    owned_one = lower_one.shape[1] // SIDE
    owned_two = lower_two.shape[1] // SIDE
    where = jnp.stack([row_index, col_index]).astype(jnp.int32)

    packed_one = pack(where, pattern_one, lower_one, capacity_one)
    rows_one = lax.all_gather(packed_one, "row", axis=0, tiled=True)
    packed_two = pack(where, pattern_two, after(lower_two, packed_one), capacity_two)
    beside_two = gather_col(packed_two)

    position_one = positions(pattern_one, row_blocks, ranks_col)
    position_two = positions(pattern_two, row_blocks, ranks_col)
    held_two = counts(pattern_two, row_blocks, ranks_col)
    base_two = jnp.concatenate([jnp.zeros((ranks_row, 1), jnp.int32), jnp.cumsum(held_two, axis=1)], axis=1)
    base_two = base_two.astype(jnp.int32)
    own_rows = lambda value: lax.dynamic_slice_in_dim(value, row_index * row_blocks, row_blocks, 0)
    own_cols = lambda value: lax.dynamic_slice_in_dim(value, col_index * col_blocks, col_blocks, 0)
    hop_one = ((jnp.arange(pattern_one.shape[1]) // owned_one) ^ col_index)[None, :]
    hop_two = ((jnp.arange(pattern_two.shape[1]) // owned_two) ^ col_index)[None, :]
    part = (jnp.arange(col_blocks) // row_blocks)[:, None]
    give_one = hop_one * capacity_one + own_rows(position_one)
    give_two = hop_two * capacity_two + own_rows(position_two)
    take_one = (hop_one * group + part) * capacity_one + own_cols(position_one)
    if turned:
        start_two = lax.dynamic_slice_in_dim(base_two, col_index, 1, 0)[:, :ranks_col]
        take_two = jnp.repeat(start_two, owned_two, axis=1) + own_cols(position_two)
    else:
        take_two = (hop_two * group + part) * capacity_two + own_cols(position_two)
    elder = (parent_two[None, :] == jnp.arange(pattern_one.shape[1])[:, None]).astype(jnp.int32)
    first_two = jnp.sum(give_one[:, :, None] * elder[None], axis=1)
    plan, table_one = make_plan(
        own_rows(pattern_one), give_one, give_one, own_cols(pattern_one), take_one
    )
    _, table_two = make_plan(own_rows(pattern_two), give_two, first_two, own_cols(pattern_two), take_two)

    link = jnp.stack(gather_col(lower_parent)).reshape(ranks_col, SIDE, owned_two * SIDE)
    link = jnp.concatenate(
        [
            lax.dynamic_index_in_dim(link, col_index ^ owner, 0, keepdims=False)
            for owner in range(ranks_col)
        ],
        axis=1,
    )
    local_ids = col_index * owned_one + jnp.arange(owned_one, dtype=jnp.int32)
    is_kid = parent_two[None, :] == local_ids[:, None]
    ids = jnp.arange(parent_two.shape[0], dtype=jnp.int32)[None, :]
    first_kid = jnp.min(jnp.where(is_kid, ids, ids.shape[1] - 1), axis=1)
    last_kid = jnp.max(jnp.where(is_kid, ids, 0), axis=1)
    kids = jnp.stack([first_kid, last_kid], axis=1).reshape(2 * owned_one)
    root = split_root(root_inverse)
    if turned:
        piece_rows = capacity_line * SIDE // (ranks_col * ranks_col)
        own_base = lax.dynamic_slice_in_dim(base_two, row_index, 1, 0)[0]
        pieces = call(
            functools.partial(line_body, ranks_col, piece_rows),
            [shape_f32(piece_rows, SIDE)] * ranks_col,
            [where, own_base],
            [*beside_two[:3], after(beside_two[3], root, table_one, table_two, link, kids)],
            [pltpu.VMEM((capacity_line * SIDE, SIDE), jnp.float32)],
        )
        ahead_two = turn(pieces)
    else:
        ahead_two = packed_two
    rows_two = lax.all_gather(ahead_two, "row", axis=0, tiled=True)
    rows_one = after(rows_one, root, ahead_two, link, table_one, table_two, kids)
    gathered_one = exchange_col(rows_one, col_index, group * capacity_one * SIDE)
    *partial_one, every_one = root_partials(
        where, plan, table_one, root, gathered_one, ranks_col, owned_one, capacity_one
    )
    mine_one, near_one, far_one, relay_one = scatter_col(partial_one)
    every_one = after(every_one, relay_one)
    known_two = call(
        functools.partial(link_body, plan),
        shape_f32(ranks_col * capacity_two * SIDE, SIDE),
        [table_two],
        [every_one, link],
    )
    far_one = after(far_one, known_two)
    off_one, inner_one, _ = call(
        functools.partial(first_body, row_blocks, ranks_col),
        [
            shape_f32(rows_here, owned_one * SIDE),
            shape_f32(3 * SIDE, owned_one * SIDE),
            shape_f32(capacity_one * SIDE, SIDE),
        ],
        [where, pattern_one, position_one, pattern_two, position_two, kids],
        [mine_one, near_one, far_one, packed_one, *beside_two],
    )
    rows_two = after(rows_two, known_two, off_one)
    if turned:
        gathered_two = rows_two
    else:
        gathered_two = exchange_col(rows_two, col_index, group * capacity_two * SIDE)
    partial_two = root_partials(
        where, plan, table_two, root, gathered_two, ranks_col, owned_two, capacity_two, known_two
    )
    *sums_two, relay_two = scatter_col(partial_two)

    inner_one = after(inner_one, relay_two)
    inner_one = sum_row(inner_one)
    diagonal_first, made = call(
        tail_body,
        [shape_f32(SIDE, owned_one * SIDE), shape_f32(2 * owned_one * SIDE, PAIR)],
        [kids],
        [diag_one, inner_one, link],
    )
    made_all = jnp.concatenate(gather_col(made), axis=0).reshape(ranks_col, owned_one, 2, SIDE, PAIR)
    chosen = []
    for local in range(owned_two):
        child = col_index * owned_two + local
        parent = lax.dynamic_index_in_dim(parent_two, child, 0, keepdims=False)
        later = jnp.sum(jnp.logical_and(parent_two == parent, ids[0] < child).astype(jnp.int32))
        hop = col_index ^ (parent // owned_one)
        chosen.append(
            lax.dynamic_slice(
                made_all, (hop, parent % owned_one, later, 0, 0), (1, 1, 1, SIDE, PAIR)
            ).reshape(SIDE, PAIR)
        )
    minus_across = jnp.concatenate([c[:, :SIDE] for c in chosen], axis=1)
    known = diag_two + jnp.concatenate([c[:, SIDE:] for c in chosen], axis=1)

    off_two, inner_two, _ = call(
        functools.partial(second_body, row_blocks),
        [
            shape_f32(rows_here, owned_two * SIDE),
            shape_f32(SIDE, owned_two * SIDE),
            shape_f32(capacity_two * SIDE, SIDE),
        ],
        [where, pattern_two, position_two],
        [*sums_two, packed_two],
    )
    return off_one, diagonal_first, off_two, minus_across, known + sum_row(inner_two)


def ladder(full_one, full_two, ranks_col):
    steps = []
    for one, two, line in ((10, 15, 52), (12, 18, 62), (16, 32, 128)):
        step = (
            rounded(one * full_one, 16) // 16,
            rounded(two * full_two, 32) // 32,
            rounded(line * full_two * ranks_col, 128) // 128,
        )
        if step not in steps:
            steps.append(step)
    return steps


def level_body(steps, row_blocks, ranks_col, one, two, level):
    def held(pattern):
        blocks, nodes = pattern.shape
        ranks_row = blocks // row_blocks
        rows = lax.broadcasted_iota(jnp.int32, (ranks_row, blocks), 0)
        inside = lax.broadcasted_iota(jnp.int32, (ranks_row, blocks), 1) // row_blocks == rows
        cols = lax.broadcasted_iota(jnp.int32, (nodes, ranks_col), 1)
        owner = lax.broadcasted_iota(jnp.int32, (nodes, ranks_col), 0) // (nodes // ranks_col) == cols
        by_row = jnp.dot(
            inside.astype(jnp.float32), pattern[...].astype(jnp.float32), preferred_element_type=jnp.float32
        )
        return jnp.dot(by_row, owner.astype(jnp.float32), preferred_element_type=jnp.float32)

    held_one, held_two = held(one), held(two)
    most = (jnp.max(held_one), jnp.max(held_two), jnp.max(jnp.sum(held_two, axis=1, keepdims=True)))
    found = jnp.int32(0)
    for step in steps[:-1]:
        over = functools.reduce(jnp.logical_or, [m > limit for m, limit in zip(most, step)])
        found = found + over.astype(jnp.int32)
    level[0] = found


def local(root_inverse, lower_one, pattern_one, diag_one, lower_two, pattern_two, *others):
    row_blocks = root_inverse.shape[0] // SIDE
    ranks_col = lax.axis_size("col")
    steps = ladder(
        row_blocks * lower_one.shape[1] // SIDE, row_blocks * lower_two.shape[1] // SIDE, ranks_col
    )
    operands = (root_inverse, lower_one, pattern_one, diag_one, lower_two, pattern_two, *others)
    if len(steps) == 1:
        return sparse_plan(steps[0], *operands)
    level = pl.pallas_call(
        functools.partial(level_body, steps, row_blocks, ranks_col),
        out_shape=jax.ShapeDtypeStruct((1,), jnp.int32),
        in_specs=[VMEM_SPEC, VMEM_SPEC],
        out_specs=SMEM_SPEC,
    )(pattern_one, pattern_two)
    return lax.switch(level[0], [functools.partial(sparse_plan, step) for step in steps], *operands)


def solution(mesh):
    return jax.shard_map(
        local,
        mesh=mesh,
        in_specs=(
            P(("pole", "row"), "col"),
            P(("pole", "row"), "col"),
            P(),
            P("pole", "col"),
            P(("pole", "row"), "col"),
            P(),
            P(),
            P("pole", "col"),
            P("pole", "col"),
        ),
        out_specs=(
            P(("pole", "row"), "col"),
            P("pole", "col"),
            P(("pole", "row"), "col"),
            P("pole", "col"),
            P("pole", "col"),
        ),
        check_vma=False,
    )
```

```python
import functools

import jax
import jax.numpy as jnp
from jax import lax
from jax.experimental import pallas as pl
from jax.experimental.pallas import tpu as pltpu
from jax.sharding import PartitionSpec as P

SIDE = 128
PAIR = 2 * SIDE
GROUP_ROWS = 2
GROUP_COLS = 4
EXACT = lax.Precision.HIGHEST
VMEM_BYTES = 56 * 1024 * 1024
ROOT_COPIES = 8

SMEM_SPEC = pl.BlockSpec(memory_space=pltpu.SMEM)
VMEM_SPEC = pl.BlockSpec(memory_space=pltpu.VMEM)
ANY_SPEC = pl.BlockSpec(memory_space=pl.ANY)


def shape_f32(rows, cols):
    return jax.ShapeDtypeStruct((rows, cols), jnp.float32)


def call(body, outs, smem, vmem, scratch=(), far=()):
    return pl.pallas_call(
        body,
        out_shape=outs,
        in_specs=[SMEM_SPEC] * len(smem) + [ANY_SPEC] * len(far) + [VMEM_SPEC] * len(vmem),
        out_specs=jax.tree.map(lambda _: VMEM_SPEC, outs),
        scratch_shapes=list(scratch),
        compiler_params=pltpu.CompilerParams(vmem_limit_bytes=VMEM_BYTES),
    )(*smem, *far, *vmem)


def halves(value):
    high = value.astype(jnp.bfloat16)
    low = (value - high.astype(jnp.float32)).astype(jnp.bfloat16)
    return high, low


def beside(value):
    return jnp.concatenate(halves(value), axis=1)


def above(value):
    return jnp.concatenate(halves(value), axis=0)


def fold_cols(value):
    return value[:, :SIDE] + value[:, SIDE:]


def fold_all(value):
    rows = value.shape[0] // 2
    return fold_cols(value[:rows] + value[rows:])


def inner(left, right):
    return fold_all(
        lax.dot_general(
            beside(left),
            beside(right),
            (((0,), (0,)), ((), ())),
            preferred_element_type=jnp.float32,
        )
    )


def block_at(index):
    return pl.ds(pl.multiple_of(index * SIDE, SIDE), SIDE)


def rounded(count, step):
    return -(-count // step) * step


def pack_body(row_blocks, where_ref, pattern, source, target):
    row_start = where_ref[0] * row_blocks
    col_index = where_ref[1]
    filled = jnp.int32(0)
    owned = source.shape[1] // SIDE
    for local in range(owned):

        def step(block, count, local=local):
            active = pattern[row_start + block, col_index * owned + local] > 0

            @pl.when(active)
            def _():
                target[block_at(count), :] = source[block_at(block), local * SIDE : (local + 1) * SIDE]

            return count + active.astype(jnp.int32)

        filled = lax.fori_loop(0, row_blocks, step, filled)


def pack(where, pattern, source, capacity):
    return call(
        functools.partial(pack_body, source.shape[0] // SIDE),
        shape_f32(capacity * SIDE, SIDE),
        [where, pattern],
        [source],
    )


def split_body(source, target):
    cols = source.shape[1]
    high, low = halves(source[...])
    target[:, :cols] = high
    target[:, cols:] = low


def split_root(root):
    rows, cols = root.shape
    step = min(rows, 256)
    return pl.pallas_call(
        split_body,
        out_shape=jax.ShapeDtypeStruct((rows, 2 * cols), jnp.bfloat16),
        grid=(rows // step,),
        in_specs=[pl.BlockSpec((step, cols), lambda i: (i, 0))],
        out_specs=pl.BlockSpec((step, 2 * cols), lambda i: (i, 0)),
        compiler_params=pltpu.CompilerParams(vmem_limit_bytes=VMEM_BYTES),
    )(root)


def line_body(ranks_col, piece_rows, where_ref, bases, *refs):
    parts, rest = refs[:ranks_col], refs[ranks_col:]
    outs, line = rest[:ranks_col], rest[ranks_col]
    col_index = where_ref[1]
    for hop in range(ranks_col):
        owner = col_index ^ hop
        base = bases[owner]

        def step(slot, carry, hop=hop, base=base):
            line[block_at(base + slot), :] = parts[hop][block_at(slot), :]
            return carry

        lax.fori_loop(0, bases[owner + 1] - base, step, jnp.int32(0))
    for step in range(ranks_col):
        at = ((col_index ^ step) * ranks_col + step) * piece_rows
        outs[step][...] = line[pl.ds(pl.multiple_of(at, 8), piece_rows), :]


class Plan:
    def __init__(self, rows, cols):
        self.rows = rounded(rows, GROUP_COLS)
        self.cols = rounded(cols, GROUP_COLS)
        self.row_block = 2
        self.row_slot = self.row_block + self.rows
        self.row_first = self.row_slot + self.rows
        self.col_block = self.row_first + self.rows
        self.col_slot = self.col_block + self.cols
        self.stride = self.col_slot + self.cols


def listed(active, values, length):
    blocks = active.shape[0]
    before = (jnp.arange(blocks)[None, :] < jnp.arange(blocks)[:, None]).astype(jnp.int32)
    rank = jnp.sum(before[:, :, None] * active[None], axis=1)
    count = jnp.sum(active, axis=0)
    wanted = jnp.minimum(jnp.arange(length)[:, None], count[None, :] - 1)
    hit = jnp.where(rank[None] == wanted[:, None, :], active[None], 0)
    return [jnp.sum(hit * value[None], axis=1).T for value in values], count


def make_plan(active_row, slot_row, first_row, active_col, slot_col):
    plan = Plan(active_row.shape[0], active_col.shape[0])
    number = lambda active: jnp.broadcast_to(jnp.arange(active.shape[0])[:, None], active.shape)
    rows, count_rows = listed(active_row, [number(active_row), slot_row, first_row], plan.rows)
    cols, count_cols = listed(active_col, [number(active_col), slot_col], plan.cols)
    table = jnp.concatenate([count_rows[:, None], count_cols[:, None], *rows, *cols], axis=1)
    return plan, table.astype(jnp.int32).reshape(-1)


def root_body(plan, ranks_col, owned, capacity, second, where_ref, table, root_ref, gathered, *refs):
    if second:
        known, *refs = refs
        outs, refs = refs[:ranks_col], refs[ranks_col:]
    else:
        outs, everything, *refs = refs[:ranks_col], *refs[ranks_col:]
    weights, root, starts, arrived = refs
    col_index = where_ref[1]
    nodes = ranks_col * owned
    cols = root.shape[1] // 2
    share = root.shape[0] // arrived.shape[0]
    copies = [
        pltpu.make_async_copy(
            root_ref.at[pl.ds(t * share, share), :], root.at[pl.ds(t * share, share), :], arrived.at[t]
        )
        for t in range(arrived.shape[0])
    ]
    for copy in copies:
        copy.start()

    def prepare(node, base):
        starts[node] = base
        at = node * plan.stride
        count = table[at + 1]

        def fill(t, carry):
            slot = table[at + plan.col_slot + t]
            weights[block_at(base + t), :] = beside(gathered[block_at(slot), :])
            return carry

        def clear(t, carry):
            weights[block_at(base + t), :] = jnp.zeros((SIDE, PAIR), jnp.bfloat16)
            return carry

        lax.fori_loop(0, count, fill, jnp.int32(0))
        upper = (count + GROUP_COLS - 1) // GROUP_COLS * GROUP_COLS
        lax.fori_loop(count, upper, clear, jnp.int32(0))
        return base + upper

    lax.fori_loop(0, nodes, prepare, jnp.int32(0))
    for copy in copies:
        copy.wait()

    def per_node(node, carry):
        at = node * plan.stride
        base = starts[node]
        hop = (node // owned) ^ col_index
        groups = (table[at + 1] + GROUP_COLS - 1) // GROUP_COLS

        def row_group(group, carry):
            blocks = [table[at + plan.row_block + group * GROUP_ROWS + t] for t in range(GROUP_ROWS)]

            def col_group(step, total):
                columns = [
                    pl.multiple_of(table[at + plan.col_block + step * GROUP_COLS + q] * SIDE, SIDE)
                    for q in range(GROUP_COLS)
                ]
                tiles = [
                    jnp.concatenate(
                        [root[block_at(block), pl.ds(shift + column, SIDE)] for column in columns], axis=1
                    )
                    for shift in (0, cols)
                    for block in blocks
                ]
                start = pl.multiple_of((base + step * GROUP_COLS) * SIDE, GROUP_COLS * SIDE)
                made = jnp.dot(
                    jnp.concatenate(tiles, axis=0),
                    weights[pl.ds(start, GROUP_COLS * SIDE), :],
                    preferred_element_type=jnp.float32,
                )
                return total + fold_all(made)

            total = lax.fori_loop(
                0, groups, col_group, jnp.zeros((GROUP_ROWS * SIDE, SIDE), jnp.float32)
            )
            for t in range(GROUP_ROWS):
                slot = table[at + plan.row_slot + group * GROUP_ROWS + t]
                value = total[t * SIDE : (t + 1) * SIDE]
                if second:
                    value = value - known[block_at(slot), :]
                else:
                    everything[block_at(slot), :] = value
                for other in range(ranks_col):

                    @pl.when(hop == other)
                    def _(other=other, slot=slot, value=value):
                        outs[other][block_at(slot - other * capacity), :] = value

            return carry

        return lax.fori_loop(0, (table[at] + GROUP_ROWS - 1) // GROUP_ROWS, row_group, carry)

    lax.fori_loop(0, nodes, per_node, jnp.int32(0))


def root_partials(where, plan, table, root, gathered, ranks_col, owned, capacity, known=None):
    rows, wide = root.shape
    nodes = ranks_col * owned
    room = min(nodes * plan.cols, rounded(gathered.shape[0] // SIDE, GROUP_COLS) + nodes * GROUP_COLS)
    copies = ROOT_COPIES if rows % (ROOT_COPIES * 16) == 0 else 1
    outs = [shape_f32(capacity * SIDE, SIDE)] * ranks_col
    if known is None:
        outs = outs + [shape_f32(ranks_col * capacity * SIDE, SIDE)]
    return call(
        functools.partial(root_body, plan, ranks_col, owned, capacity, known is not None),
        outs,
        [where, table],
        [gathered] if known is None else [gathered, known],
        [
            pltpu.VMEM((room * SIDE, PAIR), jnp.bfloat16),
            pltpu.VMEM((rows, wide), jnp.bfloat16),
            pltpu.SMEM((nodes,), jnp.int32),
            pltpu.SemaphoreType.DMA((copies,)),
        ],
        [root],
    )


def link_body(plan, table, firsts, link, out):
    nodes = link.shape[1] // SIDE

    def per_node(node, carry):
        at = node * plan.stride
        block = beside(link[:, block_at(node)])

        def step(t, carry):
            first = table[at + plan.row_first + t]
            slot = table[at + plan.row_slot + t]
            made = jnp.dot(above(firsts[block_at(first), :]), block, preferred_element_type=jnp.float32)
            out[block_at(slot), :] = fold_all(made)
            return carry

        return lax.fori_loop(0, table[at], step, carry)

    lax.fori_loop(0, nodes, per_node, jnp.int32(0))


def first_body(row_blocks, ranks_col, where_ref, pattern, position, pattern_two, position_two, kids, *refs):
    mine, near, far, packed, *rest = refs
    blocks_two, (off, sums, total) = rest[:ranks_col], rest[ranks_col:]
    row_start = where_ref[0] * row_blocks
    col_index = where_ref[1]
    owned = off.shape[1] // SIDE
    owned_two = pattern_two.shape[1] // ranks_col
    total[...] = mine[...] + near[...] + far[...]
    sums[...] = jnp.zeros(sums.shape, jnp.float32)
    for local in range(owned):
        node = col_index * owned + local
        lanes = slice(local * SIDE, (local + 1) * SIDE)

        def step(block, carry):
            place = row_start + block
            slot = position[place, node]
            active = pattern[place, node] > 0

            @pl.when(active)
            def _():
                value = total[block_at(slot), :]
                off[block_at(block), lanes] = -value
                sums[0:SIDE, lanes] += inner(packed[block_at(slot), :], value)

            @pl.when(jnp.logical_not(active))
            def _():
                off[block_at(block), lanes] = jnp.zeros((SIDE, SIDE), jnp.float32)

            for kid in range(2):
                child = kids[2 * local + kid]
                hop = col_index ^ (child // owned_two)
                slot_two = position_two[place, child]

                @pl.when(pattern_two[place, child] > 0)
                def _(kid=kid, hop=hop, slot_two=slot_two):
                    for other in range(ranks_col):

                        @pl.when(hop == other)
                        def _(other=other):
                            sums[(1 + kid) * SIDE : (2 + kid) * SIDE, lanes] += inner(
                                total[block_at(slot), :], blocks_two[other][block_at(slot_two), :]
                            )

            return carry

        lax.fori_loop(0, row_blocks, step, jnp.int32(0))


def second_body(row_blocks, where_ref, pattern, position, mine, near, far, packed, off, sums, total):
    row_start = where_ref[0] * row_blocks
    col_index = where_ref[1]
    owned = off.shape[1] // SIDE
    total[...] = mine[...] + near[...] + far[...]
    sums[...] = jnp.zeros(sums.shape, jnp.float32)
    for local in range(owned):
        node = col_index * owned + local
        lanes = slice(local * SIDE, (local + 1) * SIDE)

        def step(block, carry):
            place = row_start + block
            slot = position[place, node]
            active = pattern[place, node] > 0

            @pl.when(active)
            def _():
                value = total[block_at(slot), :]
                off[block_at(block), lanes] = -value
                sums[:, lanes] += inner(packed[block_at(slot), :], value)

            @pl.when(jnp.logical_not(active))
            def _():
                off[block_at(block), lanes] = jnp.zeros((SIDE, SIDE), jnp.float32)

            return carry

        lax.fori_loop(0, row_blocks, step, jnp.int32(0))


def tail_body(kids, diag, sums, link, diagonal, made):
    owned = diag.shape[1] // SIDE
    for local in range(owned):
        lanes = slice(local * SIDE, (local + 1) * SIDE)
        own = diag[:, lanes] + sums[0:SIDE, lanes]
        diagonal[:, lanes] = own
        for kid in range(2):
            step = link[:, block_at(kids[2 * local + kid])]
            share = sums[(1 + kid) * SIDE : (2 + kid) * SIDE, lanes]
            across = jnp.dot(own, step, precision=EXACT, preferred_element_type=jnp.float32) - share
            at = (2 * local + kid) * SIDE
            made[at : at + SIDE, 0:SIDE] = -across
            made[at : at + SIDE, SIDE:PAIR] = inner(step, across)


def swap_col(value, hop):
    ranks = lax.axis_size("col")
    return lax.ppermute(value, "col", [(c, c ^ hop) for c in range(ranks)])


def gather_col(value):
    across = swap_col(value, 2)
    return [value, swap_col(value, 1), across, swap_col(across, 1)]


def exchange_col(value, col_index, chunk):
    piece = lambda hop: lax.dynamic_slice_in_dim(value, (col_index ^ hop) * chunk, chunk, 0)
    moved = [swap_col(piece(hop), hop) for hop in (3, 2, 1)]
    return jnp.concatenate([piece(0), moved[2], moved[1], moved[0]], axis=0)


def turn(pieces):
    ranks = len(pieces)
    return jnp.concatenate(
        [
            lax.ppermute(
                piece,
                ("row", "col"),
                [(r * ranks + c, (c ^ u) * ranks + r) for r in range(ranks) for c in range(ranks)],
            )
            for u, piece in enumerate(pieces)
        ],
        axis=0,
    )


def scatter_col(parts, *before):
    relay = after(parts[2], *before) + swap_col(parts[3], 1)
    return parts[0], swap_col(parts[1], 1), swap_col(relay, 2), relay


def sum_row(value):
    ranks = lax.axis_size("row")
    reach = 1
    while reach < ranks:
        value = value + lax.ppermute(value, "row", [(r, r ^ reach) for r in range(ranks)])
        reach *= 2
    return value


def counts(pattern, row_blocks, ranks_col):
    blocks, nodes = pattern.shape
    return jnp.sum(
        pattern.reshape(blocks // row_blocks, row_blocks, ranks_col, nodes // ranks_col), axis=(1, 3)
    )


def positions(pattern, row_blocks, ranks_col):
    blocks, nodes = pattern.shape
    owned = nodes // ranks_col
    many = owned * row_blocks
    flat = (
        pattern.reshape(blocks // row_blocks, row_blocks, ranks_col, owned)
        .transpose(0, 2, 3, 1)
        .reshape(blocks // row_blocks, ranks_col, many)
    )
    before = (jnp.arange(many)[None, :] < jnp.arange(many)[:, None]).astype(jnp.int32)
    rank = jnp.sum(flat[:, :, None, :] * before[None, None], axis=-1)
    return (
        rank.reshape(blocks // row_blocks, ranks_col, owned, row_blocks)
        .transpose(0, 3, 1, 2)
        .reshape(blocks, nodes)
        .astype(jnp.int32)
    )


def after(value, *others):
    return lax.optimization_barrier((value, *others))[0]


def sparse_plan(
    capacities,
    root_inverse,
    lower_one,
    pattern_one,
    diag_one,
    lower_two,
    pattern_two,
    parent_two,
    lower_parent,
    diag_two,
):
    capacity_one, capacity_two, capacity_line = capacities
    rows_here, cols_here = root_inverse.shape
    row_blocks = rows_here // SIDE
    col_blocks = cols_here // SIDE
    ranks_row = lax.axis_size("row")
    ranks_col = lax.axis_size("col")
    turned = ranks_row == ranks_col
    group = ranks_row // ranks_col
    row_index = lax.axis_index("row")
    col_index = lax.axis_index("col")
    owned_one = lower_one.shape[1] // SIDE
    owned_two = lower_two.shape[1] // SIDE
    where = jnp.stack([row_index, col_index]).astype(jnp.int32)

    packed_one = pack(where, pattern_one, lower_one, capacity_one)
    rows_one = lax.all_gather(packed_one, "row", axis=0, tiled=True)
    packed_two = pack(where, pattern_two, after(lower_two, packed_one), capacity_two)
    beside_two = gather_col(packed_two)

    position_one = positions(pattern_one, row_blocks, ranks_col)
    position_two = positions(pattern_two, row_blocks, ranks_col)
    held_two = counts(pattern_two, row_blocks, ranks_col)
    base_two = jnp.concatenate([jnp.zeros((ranks_row, 1), jnp.int32), jnp.cumsum(held_two, axis=1)], axis=1)
    base_two = base_two.astype(jnp.int32)
    own_rows = lambda value: lax.dynamic_slice_in_dim(value, row_index * row_blocks, row_blocks, 0)
    own_cols = lambda value: lax.dynamic_slice_in_dim(value, col_index * col_blocks, col_blocks, 0)
    hop_one = ((jnp.arange(pattern_one.shape[1]) // owned_one) ^ col_index)[None, :]
    hop_two = ((jnp.arange(pattern_two.shape[1]) // owned_two) ^ col_index)[None, :]
    part = (jnp.arange(col_blocks) // row_blocks)[:, None]
    give_one = hop_one * capacity_one + own_rows(position_one)
    give_two = hop_two * capacity_two + own_rows(position_two)
    take_one = (hop_one * group + part) * capacity_one + own_cols(position_one)
    if turned:
        start_two = lax.dynamic_slice_in_dim(base_two, col_index, 1, 0)[:, :ranks_col]
        take_two = jnp.repeat(start_two, owned_two, axis=1) + own_cols(position_two)
    else:
        take_two = (hop_two * group + part) * capacity_two + own_cols(position_two)
    elder = (parent_two[None, :] == jnp.arange(pattern_one.shape[1])[:, None]).astype(jnp.int32)
    first_two = jnp.sum(give_one[:, :, None] * elder[None], axis=1)
    plan, table_one = make_plan(
        own_rows(pattern_one), give_one, give_one, own_cols(pattern_one), take_one
    )
    _, table_two = make_plan(own_rows(pattern_two), give_two, first_two, own_cols(pattern_two), take_two)

    link = jnp.stack(gather_col(lower_parent)).reshape(ranks_col, SIDE, owned_two * SIDE)
    link = jnp.concatenate(
        [
            lax.dynamic_index_in_dim(link, col_index ^ owner, 0, keepdims=False)
            for owner in range(ranks_col)
        ],
        axis=1,
    )
    local_ids = col_index * owned_one + jnp.arange(owned_one, dtype=jnp.int32)
    is_kid = parent_two[None, :] == local_ids[:, None]
    ids = jnp.arange(parent_two.shape[0], dtype=jnp.int32)[None, :]
    first_kid = jnp.min(jnp.where(is_kid, ids, ids.shape[1] - 1), axis=1)
    last_kid = jnp.max(jnp.where(is_kid, ids, 0), axis=1)
    kids = jnp.stack([first_kid, last_kid], axis=1).reshape(2 * owned_one)
    if turned:
        piece_rows = capacity_line * SIDE // (ranks_col * ranks_col)
        own_base = lax.dynamic_slice_in_dim(base_two, row_index, 1, 0)[0]
        pieces = call(
            functools.partial(line_body, ranks_col, piece_rows),
            [shape_f32(piece_rows, SIDE)] * ranks_col,
            [where, own_base],
            [*beside_two[:3], after(beside_two[3], table_one, table_two, link, kids)],
            [pltpu.VMEM((capacity_line * SIDE, SIDE), jnp.float32)],
        )
        root = split_root(after(root_inverse, *pieces))
        ahead_two = after(turn(pieces), root)
    else:
        root = split_root(root_inverse)
        ahead_two = packed_two
    rows_two = lax.all_gather(ahead_two, "row", axis=0, tiled=True)
    rows_one = after(rows_one, root, ahead_two, link, table_one, table_two, kids)
    gathered_one = exchange_col(rows_one, col_index, group * capacity_one * SIDE)
    *partial_one, every_one = root_partials(
        where, plan, table_one, root, gathered_one, ranks_col, owned_one, capacity_one
    )
    mine_one, near_one, far_one, relay_one = scatter_col(partial_one)
    every_one = after(every_one, relay_one)
    known_two = call(
        functools.partial(link_body, plan),
        shape_f32(ranks_col * capacity_two * SIDE, SIDE),
        [table_two],
        [every_one, link],
    )
    far_one = after(far_one, known_two)
    rows_two = after(rows_two, far_one)
    if turned:
        gathered_two = rows_two
    else:
        gathered_two = exchange_col(rows_two, col_index, group * capacity_two * SIDE)
    partial_two = root_partials(
        where, plan, table_two, root, gathered_two, ranks_col, owned_two, capacity_two, known_two
    )
    far_one = after(far_one, *partial_two)
    off_one, inner_one, _ = call(
        functools.partial(first_body, row_blocks, ranks_col),
        [
            shape_f32(rows_here, owned_one * SIDE),
            shape_f32(3 * SIDE, owned_one * SIDE),
            shape_f32(capacity_one * SIDE, SIDE),
        ],
        [where, pattern_one, position_one, pattern_two, position_two, kids],
        [mine_one, near_one, far_one, packed_one, *beside_two],
    )
    *sums_two, relay_two = scatter_col(partial_two, off_one)
    inner_one = sum_row(inner_one)
    diagonal_first, made = call(
        tail_body,
        [shape_f32(SIDE, owned_one * SIDE), shape_f32(2 * owned_one * SIDE, PAIR)],
        [kids],
        [diag_one, inner_one, link],
    )
    off_two, inner_two, _ = call(
        functools.partial(second_body, row_blocks),
        [
            shape_f32(rows_here, owned_two * SIDE),
            shape_f32(SIDE, owned_two * SIDE),
            shape_f32(capacity_two * SIDE, SIDE),
        ],
        [where, pattern_two, position_two],
        [*sums_two, packed_two],
    )
    made_parts = gather_col(made)
    made_parts[3] = after(made_parts[3], inner_two)
    made_all = jnp.concatenate(made_parts, axis=0).reshape(ranks_col, owned_one, 2, SIDE, PAIR)
    chosen = []
    for local in range(owned_two):
        child = col_index * owned_two + local
        parent = lax.dynamic_index_in_dim(parent_two, child, 0, keepdims=False)
        later = jnp.sum(jnp.logical_and(parent_two == parent, ids[0] < child).astype(jnp.int32))
        hop = col_index ^ (parent // owned_one)
        chosen.append(
            lax.dynamic_slice(
                made_all, (hop, parent % owned_one, later, 0, 0), (1, 1, 1, SIDE, PAIR)
            ).reshape(SIDE, PAIR)
        )
    minus_across = jnp.concatenate([c[:, :SIDE] for c in chosen], axis=1)
    known = diag_two + jnp.concatenate([c[:, SIDE:] for c in chosen], axis=1)

    return off_one, diagonal_first, off_two, minus_across, known + sum_row(inner_two)


def ladder(full_one, full_two, ranks_col):
    steps = []
    for one, two, line in ((11, 17, 56), (13, 21, 66), (16, 32, 128)):
        step = (
            rounded(one * full_one, 16) // 16,
            rounded(two * full_two, 32) // 32,
            rounded(line * full_two * ranks_col, 128) // 128,
        )
        if step not in steps:
            steps.append(step)
    return steps


def level_body(steps, row_blocks, ranks_col, one, two, level):
    def held(pattern):
        blocks, nodes = pattern.shape
        ranks_row = blocks // row_blocks
        rows = lax.broadcasted_iota(jnp.int32, (ranks_row, blocks), 0)
        inside = lax.broadcasted_iota(jnp.int32, (ranks_row, blocks), 1) // row_blocks == rows
        cols = lax.broadcasted_iota(jnp.int32, (nodes, ranks_col), 1)
        owner = lax.broadcasted_iota(jnp.int32, (nodes, ranks_col), 0) // (nodes // ranks_col) == cols
        by_row = jnp.dot(
            inside.astype(jnp.float32), pattern[...].astype(jnp.float32), preferred_element_type=jnp.float32
        )
        return jnp.dot(by_row, owner.astype(jnp.float32), preferred_element_type=jnp.float32)

    held_one, held_two = held(one), held(two)
    most = (jnp.max(held_one), jnp.max(held_two), jnp.max(jnp.sum(held_two, axis=1, keepdims=True)))
    found = jnp.int32(0)
    for step in steps[:-1]:
        over = functools.reduce(jnp.logical_or, [m > limit for m, limit in zip(most, step)])
        found = found + over.astype(jnp.int32)
    level[0] = found


def local(root_inverse, lower_one, pattern_one, diag_one, lower_two, pattern_two, *others):
    row_blocks = root_inverse.shape[0] // SIDE
    ranks_col = lax.axis_size("col")
    steps = ladder(
        row_blocks * lower_one.shape[1] // SIDE, row_blocks * lower_two.shape[1] // SIDE, ranks_col
    )
    operands = (root_inverse, lower_one, pattern_one, diag_one, lower_two, pattern_two, *others)
    if len(steps) == 1:
        return sparse_plan(steps[0], *operands)
    level = pl.pallas_call(
        functools.partial(level_body, steps, row_blocks, ranks_col),
        out_shape=jax.ShapeDtypeStruct((1,), jnp.int32),
        in_specs=[VMEM_SPEC, VMEM_SPEC],
        out_specs=SMEM_SPEC,
    )(pattern_one, pattern_two)
    return lax.switch(level[0], [functools.partial(sparse_plan, step) for step in steps], *operands)


def solution(mesh):
    return jax.shard_map(
        local,
        mesh=mesh,
        in_specs=(
            P(("pole", "row"), "col"),
            P(("pole", "row"), "col"),
            P(),
            P("pole", "col"),
            P(("pole", "row"), "col"),
            P(),
            P(),
            P("pole", "col"),
            P("pole", "col"),
        ),
        out_specs=(
            P(("pole", "row"), "col"),
            P("pole", "col"),
            P(("pole", "row"), "col"),
            P("pole", "col"),
            P("pole", "col"),
        ),
        check_vma=False,
    )
```

```python
import functools

import jax
import jax.numpy as jnp
from jax import lax
from jax.experimental import pallas as pl
from jax.experimental.pallas import tpu as pltpu
from jax.sharding import PartitionSpec as P

SIDE = 128
PAIR = 2 * SIDE
GROUP_ROWS = 2
GROUP_COLS = 4
EXACT = lax.Precision.HIGHEST
VMEM_BYTES = 56 * 1024 * 1024
ROOT_COPIES = 8

SMEM_SPEC = pl.BlockSpec(memory_space=pltpu.SMEM)
VMEM_SPEC = pl.BlockSpec(memory_space=pltpu.VMEM)
ANY_SPEC = pl.BlockSpec(memory_space=pl.ANY)


def shape_f32(rows, cols):
    return jax.ShapeDtypeStruct((rows, cols), jnp.float32)


def call(body, outs, smem, vmem, scratch=(), far=()):
    return pl.pallas_call(
        body,
        out_shape=outs,
        in_specs=[SMEM_SPEC] * len(smem) + [ANY_SPEC] * len(far) + [VMEM_SPEC] * len(vmem),
        out_specs=jax.tree.map(lambda _: VMEM_SPEC, outs),
        scratch_shapes=list(scratch),
        compiler_params=pltpu.CompilerParams(vmem_limit_bytes=VMEM_BYTES),
    )(*smem, *far, *vmem)


def halves(value):
    high = value.astype(jnp.bfloat16)
    low = (value - high.astype(jnp.float32)).astype(jnp.bfloat16)
    return high, low


def beside(value):
    return jnp.concatenate(halves(value), axis=1)


def above(value):
    return jnp.concatenate(halves(value), axis=0)


def fold_cols(value):
    return value[:, :SIDE] + value[:, SIDE:]


def fold_all(value):
    rows = value.shape[0] // 2
    return fold_cols(value[:rows] + value[rows:])


def inner(left, right):
    return fold_all(
        lax.dot_general(
            beside(left),
            beside(right),
            (((0,), (0,)), ((), ())),
            preferred_element_type=jnp.float32,
        )
    )


def block_at(index):
    return pl.ds(pl.multiple_of(index * SIDE, SIDE), SIDE)


def rounded(count, step):
    return -(-count // step) * step


def pack_body(row_blocks, where_ref, pattern, source, target):
    row_start = where_ref[0] * row_blocks
    col_index = where_ref[1]
    filled = jnp.int32(0)
    owned = source.shape[1] // SIDE
    for local in range(owned):

        def step(block, count, local=local):
            active = pattern[row_start + block, col_index * owned + local] > 0

            @pl.when(active)
            def _():
                target[block_at(count), :] = source[block_at(block), local * SIDE : (local + 1) * SIDE]

            return count + active.astype(jnp.int32)

        filled = lax.fori_loop(0, row_blocks, step, filled)


def pack(where, pattern, source, capacity):
    return call(
        functools.partial(pack_body, source.shape[0] // SIDE),
        shape_f32(capacity * SIDE, SIDE),
        [where, pattern],
        [source],
    )


def split_body(source, target):
    cols = source.shape[1]
    high, low = halves(source[...])
    target[:, :cols] = high
    target[:, cols:] = low


def split_root(root):
    rows, cols = root.shape
    step = min(rows, 256)
    return pl.pallas_call(
        split_body,
        out_shape=jax.ShapeDtypeStruct((rows, 2 * cols), jnp.bfloat16),
        grid=(rows // step,),
        in_specs=[pl.BlockSpec((step, cols), lambda i: (i, 0))],
        out_specs=pl.BlockSpec((step, 2 * cols), lambda i: (i, 0)),
        compiler_params=pltpu.CompilerParams(vmem_limit_bytes=VMEM_BYTES),
    )(root)


def line_body(ranks_col, piece_rows, where_ref, bases, *refs):
    parts, rest = refs[:ranks_col], refs[ranks_col:]
    outs, line = rest[:ranks_col], rest[ranks_col]
    col_index = where_ref[1]
    for hop in range(ranks_col):
        owner = col_index ^ hop
        base = bases[owner]

        def step(slot, carry, hop=hop, base=base):
            line[block_at(base + slot), :] = parts[hop][block_at(slot), :]
            return carry

        lax.fori_loop(0, bases[owner + 1] - base, step, jnp.int32(0))
    for step in range(ranks_col):
        at = ((col_index ^ step) * ranks_col + step) * piece_rows
        outs[step][...] = line[pl.ds(pl.multiple_of(at, 8), piece_rows), :]


class Plan:
    def __init__(self, rows, cols):
        self.rows = rounded(rows, GROUP_COLS)
        self.cols = rounded(cols, GROUP_COLS)
        self.row_block = 2
        self.row_slot = self.row_block + self.rows
        self.row_first = self.row_slot + self.rows
        self.col_block = self.row_first + self.rows
        self.col_slot = self.col_block + self.cols
        self.stride = self.col_slot + self.cols


def listed(active, values, length):
    blocks = active.shape[0]
    before = (jnp.arange(blocks)[None, :] < jnp.arange(blocks)[:, None]).astype(jnp.int32)
    rank = jnp.sum(before[:, :, None] * active[None], axis=1)
    count = jnp.sum(active, axis=0)
    wanted = jnp.minimum(jnp.arange(length)[:, None], count[None, :] - 1)
    hit = jnp.where(rank[None] == wanted[:, None, :], active[None], 0)
    return [jnp.sum(hit * value[None], axis=1).T for value in values], count


def make_plan(active_row, slot_row, first_row, active_col, slot_col):
    plan = Plan(active_row.shape[0], active_col.shape[0])
    number = lambda active: jnp.broadcast_to(jnp.arange(active.shape[0])[:, None], active.shape)
    rows, count_rows = listed(active_row, [number(active_row), slot_row, first_row], plan.rows)
    cols, count_cols = listed(active_col, [number(active_col), slot_col], plan.cols)
    table = jnp.concatenate([count_rows[:, None], count_cols[:, None], *rows, *cols], axis=1)
    return plan, table.astype(jnp.int32).reshape(-1)


def root_body(plan, hops, owned, capacity, second, where_ref, table, root_ref, gathered, *refs):
    if second:
        known, *refs = refs
        outs, refs = refs[: len(hops)], refs[len(hops) :]
    else:
        outs, everything, *refs = refs[: len(hops)], *refs[len(hops) :]
    weights, root, starts, arrived = refs
    col_index = where_ref[1]
    jobs = len(hops) * owned
    cols = root.shape[1] // 2

    def place_of(job):
        hop = hops[0] + job // owned
        return hop, ((hop ^ col_index) * owned + job % owned) * plan.stride

    share = root.shape[0] // arrived.shape[0]
    copies = [
        pltpu.make_async_copy(
            root_ref.at[pl.ds(t * share, share), :], root.at[pl.ds(t * share, share), :], arrived.at[t]
        )
        for t in range(arrived.shape[0])
    ]
    for copy in copies:
        copy.start()

    def prepare(job, base):
        starts[job] = base
        _, at = place_of(job)
        count = table[at + 1]

        def fill(t, carry):
            slot = table[at + plan.col_slot + t]
            weights[block_at(base + t), :] = beside(gathered[block_at(slot), :])
            return carry

        def clear(t, carry):
            weights[block_at(base + t), :] = jnp.zeros((SIDE, PAIR), jnp.bfloat16)
            return carry

        lax.fori_loop(0, count, fill, jnp.int32(0))
        upper = (count + GROUP_COLS - 1) // GROUP_COLS * GROUP_COLS
        lax.fori_loop(count, upper, clear, jnp.int32(0))
        return base + upper

    lax.fori_loop(0, jobs, prepare, jnp.int32(0))
    for copy in copies:
        copy.wait()

    def per_job(job, carry):
        hop, at = place_of(job)
        base = starts[job]
        groups = (table[at + 1] + GROUP_COLS - 1) // GROUP_COLS

        def row_group(group, carry):
            blocks = [table[at + plan.row_block + group * GROUP_ROWS + t] for t in range(GROUP_ROWS)]

            def col_group(step, total):
                columns = [
                    pl.multiple_of(table[at + plan.col_block + step * GROUP_COLS + q] * SIDE, SIDE)
                    for q in range(GROUP_COLS)
                ]
                tiles = [
                    jnp.concatenate(
                        [root[block_at(block), pl.ds(shift + column, SIDE)] for column in columns], axis=1
                    )
                    for shift in (0, cols)
                    for block in blocks
                ]
                start = pl.multiple_of((base + step * GROUP_COLS) * SIDE, GROUP_COLS * SIDE)
                made = jnp.dot(
                    jnp.concatenate(tiles, axis=0),
                    weights[pl.ds(start, GROUP_COLS * SIDE), :],
                    preferred_element_type=jnp.float32,
                )
                return total + fold_all(made)

            total = lax.fori_loop(
                0, groups, col_group, jnp.zeros((GROUP_ROWS * SIDE, SIDE), jnp.float32)
            )
            for t in range(GROUP_ROWS):
                slot = table[at + plan.row_slot + group * GROUP_ROWS + t]
                value = total[t * SIDE : (t + 1) * SIDE]
                if second:
                    value = value - known[block_at(slot), :]
                else:
                    everything[block_at(slot), :] = value
                for out, other in zip(outs, hops):

                    @pl.when(hop == other)
                    def _(out=out, other=other, slot=slot, value=value):
                        out[block_at(slot - other * capacity), :] = value

            return carry

        return lax.fori_loop(0, (table[at] + GROUP_ROWS - 1) // GROUP_ROWS, row_group, carry)

    lax.fori_loop(0, jobs, per_job, jnp.int32(0))


def root_partials(where, plan, table, root, gathered, hops, owned, capacity, known=None):
    rows, wide = root.shape
    nodes = len(hops) * owned
    room = min(nodes * plan.cols, rounded(gathered.shape[0] // SIDE, GROUP_COLS) + nodes * GROUP_COLS)
    copies = ROOT_COPIES if rows % (ROOT_COPIES * 16) == 0 else 1
    outs = [shape_f32(capacity * SIDE, SIDE)] * len(hops)
    if known is None:
        outs = outs + [shape_f32(len(hops) * capacity * SIDE, SIDE)]
    return call(
        functools.partial(root_body, plan, hops, owned, capacity, known is not None),
        outs,
        [where, table],
        [gathered] if known is None else [gathered, known],
        [
            pltpu.VMEM((room * SIDE, PAIR), jnp.bfloat16),
            pltpu.VMEM((rows, wide), jnp.bfloat16),
            pltpu.SMEM((nodes,), jnp.int32),
            pltpu.SemaphoreType.DMA((copies,)),
        ],
        [root],
    )


def link_body(plan, table, firsts, link, out):
    nodes = link.shape[1] // SIDE

    def per_node(node, carry):
        at = node * plan.stride
        block = beside(link[:, block_at(node)])

        def step(t, carry):
            first = table[at + plan.row_first + t]
            slot = table[at + plan.row_slot + t]
            made = jnp.dot(above(firsts[block_at(first), :]), block, preferred_element_type=jnp.float32)
            out[block_at(slot), :] = fold_all(made)
            return carry

        return lax.fori_loop(0, table[at], step, carry)

    lax.fori_loop(0, nodes, per_node, jnp.int32(0))


def first_body(row_blocks, ranks_col, where_ref, pattern, position, pattern_two, position_two, kids, *refs):
    mine, near, far, packed, *rest = refs
    blocks_two, (off, sums, total) = rest[:ranks_col], rest[ranks_col:]
    row_start = where_ref[0] * row_blocks
    col_index = where_ref[1]
    owned = off.shape[1] // SIDE
    owned_two = pattern_two.shape[1] // ranks_col
    total[...] = mine[...] + near[...] + far[...]
    sums[...] = jnp.zeros(sums.shape, jnp.float32)
    for local in range(owned):
        node = col_index * owned + local
        lanes = slice(local * SIDE, (local + 1) * SIDE)

        def step(block, carry):
            place = row_start + block
            slot = position[place, node]
            active = pattern[place, node] > 0

            @pl.when(active)
            def _():
                value = total[block_at(slot), :]
                off[block_at(block), lanes] = -value
                sums[0:SIDE, lanes] += inner(packed[block_at(slot), :], value)

            @pl.when(jnp.logical_not(active))
            def _():
                off[block_at(block), lanes] = jnp.zeros((SIDE, SIDE), jnp.float32)

            for kid in range(2):
                child = kids[2 * local + kid]
                hop = col_index ^ (child // owned_two)
                slot_two = position_two[place, child]

                @pl.when(pattern_two[place, child] > 0)
                def _(kid=kid, hop=hop, slot_two=slot_two):
                    for other in range(ranks_col):

                        @pl.when(hop == other)
                        def _(other=other):
                            sums[(1 + kid) * SIDE : (2 + kid) * SIDE, lanes] += inner(
                                total[block_at(slot), :], blocks_two[other][block_at(slot_two), :]
                            )

            return carry

        lax.fori_loop(0, row_blocks, step, jnp.int32(0))


def second_body(row_blocks, where_ref, pattern, position, mine, near, far, packed, off, sums, total):
    row_start = where_ref[0] * row_blocks
    col_index = where_ref[1]
    owned = off.shape[1] // SIDE
    total[...] = mine[...] + near[...] + far[...]
    sums[...] = jnp.zeros(sums.shape, jnp.float32)
    for local in range(owned):
        node = col_index * owned + local
        lanes = slice(local * SIDE, (local + 1) * SIDE)

        def step(block, carry):
            place = row_start + block
            slot = position[place, node]
            active = pattern[place, node] > 0

            @pl.when(active)
            def _():
                value = total[block_at(slot), :]
                off[block_at(block), lanes] = -value
                sums[:, lanes] += inner(packed[block_at(slot), :], value)

            @pl.when(jnp.logical_not(active))
            def _():
                off[block_at(block), lanes] = jnp.zeros((SIDE, SIDE), jnp.float32)

            return carry

        lax.fori_loop(0, row_blocks, step, jnp.int32(0))


def tail_body(kids, diag, sums, link, diagonal, made):
    owned = diag.shape[1] // SIDE
    for local in range(owned):
        lanes = slice(local * SIDE, (local + 1) * SIDE)
        own = diag[:, lanes] + sums[0:SIDE, lanes]
        diagonal[:, lanes] = own
        for kid in range(2):
            step = link[:, block_at(kids[2 * local + kid])]
            share = sums[(1 + kid) * SIDE : (2 + kid) * SIDE, lanes]
            across = jnp.dot(own, step, precision=EXACT, preferred_element_type=jnp.float32) - share
            at = (2 * local + kid) * SIDE
            made[at : at + SIDE, 0:SIDE] = -across
            made[at : at + SIDE, SIDE:PAIR] = inner(step, across)


def swap_col(value, hop):
    ranks = lax.axis_size("col")
    return lax.ppermute(value, "col", [(c, c ^ hop) for c in range(ranks)])


def gather_col(value, *before):
    across = after(swap_col(value, 2), *before)
    return [value, swap_col(value, 1), across, swap_col(across, 1)]


def exchange_col(value, col_index, chunk):
    piece = lambda hop: lax.dynamic_slice_in_dim(value, (col_index ^ hop) * chunk, chunk, 0)
    moved = [swap_col(piece(hop), hop) for hop in (3, 2, 1)]
    return jnp.concatenate([piece(0), moved[2], moved[1], moved[0]], axis=0)


def turn(pieces):
    ranks = len(pieces)
    return jnp.concatenate(
        [
            lax.ppermute(
                piece,
                ("row", "col"),
                [(r * ranks + c, (c ^ u) * ranks + r) for r in range(ranks) for c in range(ranks)],
            )
            for u, piece in enumerate(pieces)
        ],
        axis=0,
    )


def scatter_col(parts):
    relay = parts[2] + swap_col(parts[3], 1)
    return parts[0], swap_col(parts[1], 1), swap_col(relay, 2), relay


def sum_row(value):
    ranks = lax.axis_size("row")
    reach = 1
    while reach < ranks:
        value = value + lax.ppermute(value, "row", [(r, r ^ reach) for r in range(ranks)])
        reach *= 2
    return value


def counts(pattern, row_blocks, ranks_col):
    blocks, nodes = pattern.shape
    return jnp.sum(
        pattern.reshape(blocks // row_blocks, row_blocks, ranks_col, nodes // ranks_col), axis=(1, 3)
    )


def positions(pattern, row_blocks, ranks_col):
    blocks, nodes = pattern.shape
    owned = nodes // ranks_col
    many = owned * row_blocks
    flat = (
        pattern.reshape(blocks // row_blocks, row_blocks, ranks_col, owned)
        .transpose(0, 2, 3, 1)
        .reshape(blocks // row_blocks, ranks_col, many)
    )
    before = (jnp.arange(many)[None, :] < jnp.arange(many)[:, None]).astype(jnp.int32)
    rank = jnp.sum(flat[:, :, None, :] * before[None, None], axis=-1)
    return (
        rank.reshape(blocks // row_blocks, ranks_col, owned, row_blocks)
        .transpose(0, 3, 1, 2)
        .reshape(blocks, nodes)
        .astype(jnp.int32)
    )


def after(value, *others):
    return lax.optimization_barrier((value, *others))[0]


def sparse_plan(
    capacities,
    root_inverse,
    lower_one,
    pattern_one,
    diag_one,
    lower_two,
    pattern_two,
    parent_two,
    lower_parent,
    diag_two,
):
    capacity_one, capacity_two, capacity_line = capacities
    rows_here, cols_here = root_inverse.shape
    row_blocks = rows_here // SIDE
    col_blocks = cols_here // SIDE
    ranks_row = lax.axis_size("row")
    ranks_col = lax.axis_size("col")
    turned = ranks_row == ranks_col
    group = ranks_row // ranks_col
    row_index = lax.axis_index("row")
    col_index = lax.axis_index("col")
    owned_one = lower_one.shape[1] // SIDE
    owned_two = lower_two.shape[1] // SIDE
    where = jnp.stack([row_index, col_index]).astype(jnp.int32)

    packed_one = pack(where, pattern_one, lower_one, capacity_one)
    rows_one = lax.all_gather(packed_one, "row", axis=0, tiled=True)
    packed_two = pack(where, pattern_two, after(lower_two, packed_one), capacity_two)

    position_one = positions(pattern_one, row_blocks, ranks_col)
    position_two = positions(pattern_two, row_blocks, ranks_col)
    held_two = counts(pattern_two, row_blocks, ranks_col)
    base_two = jnp.concatenate([jnp.zeros((ranks_row, 1), jnp.int32), jnp.cumsum(held_two, axis=1)], axis=1)
    base_two = base_two.astype(jnp.int32)
    own_rows = lambda value: lax.dynamic_slice_in_dim(value, row_index * row_blocks, row_blocks, 0)
    own_cols = lambda value: lax.dynamic_slice_in_dim(value, col_index * col_blocks, col_blocks, 0)
    hop_one = ((jnp.arange(pattern_one.shape[1]) // owned_one) ^ col_index)[None, :]
    hop_two = ((jnp.arange(pattern_two.shape[1]) // owned_two) ^ col_index)[None, :]
    part = (jnp.arange(col_blocks) // row_blocks)[:, None]
    give_one = hop_one * capacity_one + own_rows(position_one)
    give_two = hop_two * capacity_two + own_rows(position_two)
    take_one = (hop_one * group + part) * capacity_one + own_cols(position_one)
    if turned:
        start_two = lax.dynamic_slice_in_dim(base_two, col_index, 1, 0)[:, :ranks_col]
        take_two = jnp.repeat(start_two, owned_two, axis=1) + own_cols(position_two)
    else:
        take_two = (hop_two * group + part) * capacity_two + own_cols(position_two)
    elder = (parent_two[None, :] == jnp.arange(pattern_one.shape[1])[:, None]).astype(jnp.int32)
    first_two = jnp.sum(give_one[:, :, None] * elder[None], axis=1)
    plan, table_one = make_plan(
        own_rows(pattern_one), give_one, give_one, own_cols(pattern_one), take_one
    )
    _, table_two = make_plan(own_rows(pattern_two), give_two, first_two, own_cols(pattern_two), take_two)

    local_ids = col_index * owned_one + jnp.arange(owned_one, dtype=jnp.int32)
    is_kid = parent_two[None, :] == local_ids[:, None]
    ids = jnp.arange(parent_two.shape[0], dtype=jnp.int32)[None, :]
    first_kid = jnp.min(jnp.where(is_kid, ids, ids.shape[1] - 1), axis=1)
    last_kid = jnp.max(jnp.where(is_kid, ids, 0), axis=1)
    kids = jnp.stack([first_kid, last_kid], axis=1).reshape(2 * owned_one)
    beside_two = gather_col(packed_two, table_one, table_two, kids)
    link = jnp.stack(gather_col(after(lower_parent, packed_two))).reshape(ranks_col, SIDE, owned_two * SIDE)
    link = jnp.concatenate(
        [
            lax.dynamic_index_in_dim(link, col_index ^ owner, 0, keepdims=False)
            for owner in range(ranks_col)
        ],
        axis=1,
    )
    if turned:
        piece_rows = capacity_line * SIDE // (ranks_col * ranks_col)
        own_base = lax.dynamic_slice_in_dim(base_two, row_index, 1, 0)[0]
        pieces = call(
            functools.partial(line_body, ranks_col, piece_rows),
            [shape_f32(piece_rows, SIDE)] * ranks_col,
            [where, own_base],
            beside_two,
            [pltpu.VMEM((capacity_line * SIDE, SIDE), jnp.float32)],
        )
        root = split_root(after(root_inverse, *pieces))
        ahead_two = after(turn(pieces), root)
    else:
        root = split_root(root_inverse)
        ahead_two = packed_two
    rows_two = lax.all_gather(ahead_two, "row", axis=0, tiled=True)
    rows_one = after(rows_one, root, ahead_two)
    gathered_one = exchange_col(rows_one, col_index, group * capacity_one * SIDE)
    *partial_one, every_one = root_partials(
        where, plan, table_one, after(root, link), gathered_one, range(ranks_col), owned_one, capacity_one
    )
    mine_one, near_one, far_one, relay_one = scatter_col(partial_one)
    every_one = after(every_one, relay_one)
    known_two = call(
        functools.partial(link_body, plan),
        shape_f32(ranks_col * capacity_two * SIDE, SIDE),
        [table_two],
        [every_one, link],
    )
    far_one = after(far_one, known_two)
    rows_two = after(rows_two, far_one)
    if turned:
        gathered_two = rows_two
    else:
        gathered_two = exchange_col(rows_two, col_index, group * capacity_two * SIDE)
    partial_two = root_partials(
        where, plan, table_two, root, gathered_two, range(ranks_col), owned_two, capacity_two, known_two
    )
    far_one = after(far_one, *partial_two)
    off_one, inner_one, _ = call(
        functools.partial(first_body, row_blocks, ranks_col),
        [
            shape_f32(rows_here, owned_one * SIDE),
            shape_f32(3 * SIDE, owned_one * SIDE),
            shape_f32(capacity_one * SIDE, SIDE),
        ],
        [where, pattern_one, position_one, pattern_two, position_two, kids],
        [mine_one, near_one, far_one, packed_one, *beside_two],
    )
    relay_two = after(partial_two[2], off_one) + swap_col(partial_two[3], 1)
    sums_two = [partial_two[0], swap_col(partial_two[1], 1), swap_col(relay_two, 2)]
    inner_one = sum_row(inner_one)
    diagonal_first, made = call(
        tail_body,
        [shape_f32(SIDE, owned_one * SIDE), shape_f32(2 * owned_one * SIDE, PAIR)],
        [kids],
        [diag_one, inner_one, link],
    )
    off_two, inner_two, _ = call(
        functools.partial(second_body, row_blocks),
        [
            shape_f32(rows_here, owned_two * SIDE),
            shape_f32(SIDE, owned_two * SIDE),
            shape_f32(capacity_two * SIDE, SIDE),
        ],
        [where, pattern_two, position_two],
        [*sums_two, packed_two],
    )
    made_parts = gather_col(made, inner_two)
    made_all = jnp.concatenate(made_parts, axis=0).reshape(ranks_col, owned_one, 2, SIDE, PAIR)
    chosen = []
    for local in range(owned_two):
        child = col_index * owned_two + local
        parent = lax.dynamic_index_in_dim(parent_two, child, 0, keepdims=False)
        later = jnp.sum(jnp.logical_and(parent_two == parent, ids[0] < child).astype(jnp.int32))
        hop = col_index ^ (parent // owned_one)
        chosen.append(
            lax.dynamic_slice(
                made_all, (hop, parent % owned_one, later, 0, 0), (1, 1, 1, SIDE, PAIR)
            ).reshape(SIDE, PAIR)
        )
    minus_across = jnp.concatenate([c[:, :SIDE] for c in chosen], axis=1)
    known = diag_two + jnp.concatenate([c[:, SIDE:] for c in chosen], axis=1)

    return off_one, diagonal_first, off_two, minus_across, known + sum_row(inner_two)


def ladder(full_one, full_two, ranks_col):
    steps = []
    for one, two, line in ((11, 17, 56), (13, 21, 66), (16, 32, 128)):
        step = (
            rounded(one * full_one, 16) // 16,
            rounded(two * full_two, 32) // 32,
            rounded(line * full_two * ranks_col, 128) // 128,
        )
        if step not in steps:
            steps.append(step)
    return steps


def level_body(steps, row_blocks, ranks_col, one, two, level):
    def held(pattern):
        blocks, nodes = pattern.shape
        ranks_row = blocks // row_blocks
        rows = lax.broadcasted_iota(jnp.int32, (ranks_row, blocks), 0)
        inside = lax.broadcasted_iota(jnp.int32, (ranks_row, blocks), 1) // row_blocks == rows
        cols = lax.broadcasted_iota(jnp.int32, (nodes, ranks_col), 1)
        owner = lax.broadcasted_iota(jnp.int32, (nodes, ranks_col), 0) // (nodes // ranks_col) == cols
        by_row = jnp.dot(
            inside.astype(jnp.float32), pattern[...].astype(jnp.float32), preferred_element_type=jnp.float32
        )
        return jnp.dot(by_row, owner.astype(jnp.float32), preferred_element_type=jnp.float32)

    held_one, held_two = held(one), held(two)
    most = (jnp.max(held_one), jnp.max(held_two), jnp.max(jnp.sum(held_two, axis=1, keepdims=True)))
    found = jnp.int32(0)
    for step in steps[:-1]:
        over = functools.reduce(jnp.logical_or, [m > limit for m, limit in zip(most, step)])
        found = found + over.astype(jnp.int32)
    level[0] = found


def local(root_inverse, lower_one, pattern_one, diag_one, lower_two, pattern_two, *others):
    row_blocks = root_inverse.shape[0] // SIDE
    ranks_col = lax.axis_size("col")
    steps = ladder(
        row_blocks * lower_one.shape[1] // SIDE, row_blocks * lower_two.shape[1] // SIDE, ranks_col
    )
    operands = (root_inverse, lower_one, pattern_one, diag_one, lower_two, pattern_two, *others)
    if len(steps) == 1:
        return sparse_plan(steps[0], *operands)
    level = pl.pallas_call(
        functools.partial(level_body, steps, row_blocks, ranks_col),
        out_shape=jax.ShapeDtypeStruct((1,), jnp.int32),
        in_specs=[VMEM_SPEC, VMEM_SPEC],
        out_specs=SMEM_SPEC,
    )(pattern_one, pattern_two)
    return lax.switch(level[0], [functools.partial(sparse_plan, step) for step in steps], *operands)


def solution(mesh):
    return jax.shard_map(
        local,
        mesh=mesh,
        in_specs=(
            P(("pole", "row"), "col"),
            P(("pole", "row"), "col"),
            P(),
            P("pole", "col"),
            P(("pole", "row"), "col"),
            P(),
            P(),
            P("pole", "col"),
            P("pole", "col"),
        ),
        out_specs=(
            P(("pole", "row"), "col"),
            P("pole", "col"),
            P(("pole", "row"), "col"),
            P("pole", "col"),
            P("pole", "col"),
        ),
        check_vma=False,
    )
```

```python
import functools

import jax
import jax.numpy as jnp
from jax import lax
from jax.experimental import pallas as pl
from jax.experimental.pallas import tpu as pltpu
from jax.sharding import PartitionSpec as P

SIDE = 128
PAIR = 2 * SIDE
GROUP_ROWS = 4
GROUP_COLS = 4
EXACT = lax.Precision.HIGHEST
VMEM_BYTES = 56 * 1024 * 1024
ROOT_COPIES = 8

SMEM_SPEC = pl.BlockSpec(memory_space=pltpu.SMEM)
VMEM_SPEC = pl.BlockSpec(memory_space=pltpu.VMEM)
ANY_SPEC = pl.BlockSpec(memory_space=pl.ANY)


def shape_f32(rows, cols):
    return jax.ShapeDtypeStruct((rows, cols), jnp.float32)


def call(body, outs, smem, vmem, scratch=(), far=()):
    return pl.pallas_call(
        body,
        out_shape=outs,
        in_specs=[SMEM_SPEC] * len(smem) + [ANY_SPEC] * len(far) + [VMEM_SPEC] * len(vmem),
        out_specs=jax.tree.map(lambda _: VMEM_SPEC, outs),
        scratch_shapes=list(scratch),
        compiler_params=pltpu.CompilerParams(vmem_limit_bytes=VMEM_BYTES),
    )(*smem, *far, *vmem)


def halves(value):
    high = value.astype(jnp.bfloat16)
    low = (value - high.astype(jnp.float32)).astype(jnp.bfloat16)
    return high, low


def beside(value):
    return jnp.concatenate(halves(value), axis=1)


def above(value):
    return jnp.concatenate(halves(value), axis=0)


def fold_cols(value):
    return value[:, :SIDE] + value[:, SIDE:]


def fold_all(value):
    rows = value.shape[0] // 2
    return fold_cols(value[:rows] + value[rows:])


def inner(left, right):
    return fold_all(
        lax.dot_general(
            beside(left),
            beside(right),
            (((0,), (0,)), ((), ())),
            preferred_element_type=jnp.float32,
        )
    )


def block_at(index):
    return pl.ds(pl.multiple_of(index * SIDE, SIDE), SIDE)


def rounded(count, step):
    return -(-count // step) * step


def pack_body(row_blocks, where_ref, pattern, source, target):
    row_start = where_ref[0] * row_blocks
    col_index = where_ref[1]
    filled = jnp.int32(0)
    owned = source.shape[1] // SIDE
    for local in range(owned):

        def step(block, count, local=local):
            active = pattern[row_start + block, col_index * owned + local] > 0

            @pl.when(active)
            def _():
                target[block_at(count), :] = source[block_at(block), local * SIDE : (local + 1) * SIDE]

            return count + active.astype(jnp.int32)

        filled = lax.fori_loop(0, row_blocks, step, filled)


def pack(where, pattern, source, capacity):
    return call(
        functools.partial(pack_body, source.shape[0] // SIDE),
        shape_f32(capacity * SIDE, SIDE),
        [where, pattern],
        [source],
    )


def split_body(source, target):
    cols = source.shape[1]
    high, low = halves(source[...])
    target[:, :cols] = high
    target[:, cols:] = low


def split_root(root):
    rows, cols = root.shape
    step = min(rows, 256)
    return pl.pallas_call(
        split_body,
        out_shape=jax.ShapeDtypeStruct((rows, 2 * cols), jnp.bfloat16),
        grid=(rows // step,),
        in_specs=[pl.BlockSpec((step, cols), lambda i: (i, 0))],
        out_specs=pl.BlockSpec((step, 2 * cols), lambda i: (i, 0)),
        compiler_params=pltpu.CompilerParams(vmem_limit_bytes=VMEM_BYTES),
    )(root)


def line_body(ranks_col, piece_rows, where_ref, bases, *refs):
    parts, rest = refs[:ranks_col], refs[ranks_col:]
    outs, line = rest[:ranks_col], rest[ranks_col]
    col_index = where_ref[1]
    for hop in range(ranks_col):
        owner = col_index ^ hop
        base = bases[owner]

        def step(slot, carry, hop=hop, base=base):
            line[block_at(base + slot), :] = parts[hop][block_at(slot), :]
            return carry

        lax.fori_loop(0, bases[owner + 1] - base, step, jnp.int32(0))
    for step in range(ranks_col):
        at = ((col_index ^ step) * ranks_col + step) * piece_rows
        outs[step][...] = line[pl.ds(pl.multiple_of(at, 8), piece_rows), :]


class Plan:
    def __init__(self, rows, cols):
        self.rows = rounded(rows, GROUP_COLS)
        self.cols = rounded(cols, GROUP_COLS)
        self.row_block = 2
        self.row_slot = self.row_block + self.rows
        self.row_first = self.row_slot + self.rows
        self.col_block = self.row_first + self.rows
        self.col_slot = self.col_block + self.cols
        self.stride = self.col_slot + self.cols


def listed(active, values, length):
    blocks = active.shape[0]
    before = (jnp.arange(blocks)[None, :] < jnp.arange(blocks)[:, None]).astype(jnp.int32)
    rank = jnp.sum(before[:, :, None] * active[None], axis=1)
    count = jnp.sum(active, axis=0)
    wanted = jnp.minimum(jnp.arange(length)[:, None], count[None, :] - 1)
    hit = jnp.where(rank[None] == wanted[:, None, :], active[None], 0)
    return [jnp.sum(hit * value[None], axis=1).T for value in values], count


def make_plan(active_row, slot_row, first_row, active_col, slot_col):
    plan = Plan(active_row.shape[0], active_col.shape[0])
    number = lambda active: jnp.broadcast_to(jnp.arange(active.shape[0])[:, None], active.shape)
    rows, count_rows = listed(active_row, [number(active_row), slot_row, first_row], plan.rows)
    cols, count_cols = listed(active_col, [number(active_col), slot_col], plan.cols)
    table = jnp.concatenate([count_rows[:, None], count_cols[:, None], *rows, *cols], axis=1)
    return plan, table.astype(jnp.int32).reshape(-1)


def root_body(plan, hops, owned, capacity, second, where_ref, table, root_ref, gathered, *refs):
    if second:
        known, *refs = refs
        outs, refs = refs[: len(hops)], refs[len(hops) :]
    else:
        outs, everything, *refs = refs[: len(hops)], *refs[len(hops) :]
    weights, root, starts, arrived = refs
    col_index = where_ref[1]
    jobs = len(hops) * owned
    cols = root.shape[1] // 2

    def place_of(job):
        hop = hops[0] + job // owned
        return hop, ((hop ^ col_index) * owned + job % owned) * plan.stride

    share = root.shape[0] // arrived.shape[0]
    copies = [
        pltpu.make_async_copy(
            root_ref.at[pl.ds(t * share, share), :], root.at[pl.ds(t * share, share), :], arrived.at[t]
        )
        for t in range(arrived.shape[0])
    ]
    for copy in copies:
        copy.start()

    def prepare(job, base):
        starts[job] = base
        _, at = place_of(job)
        count = table[at + 1]

        def fill(t, carry):
            slot = table[at + plan.col_slot + t]
            weights[block_at(base + t), :] = beside(gathered[block_at(slot), :])
            return carry

        def clear(t, carry):
            weights[block_at(base + t), :] = jnp.zeros((SIDE, PAIR), jnp.bfloat16)
            return carry

        lax.fori_loop(0, count, fill, jnp.int32(0))
        upper = (count + GROUP_COLS - 1) // GROUP_COLS * GROUP_COLS
        lax.fori_loop(count, upper, clear, jnp.int32(0))
        return base + upper

    lax.fori_loop(0, jobs, prepare, jnp.int32(0))
    for copy in copies:
        copy.wait()

    def per_job(job, carry):
        hop, at = place_of(job)
        base = starts[job]
        groups = (table[at + 1] + GROUP_COLS - 1) // GROUP_COLS

        def row_group(group, carry):
            blocks = [table[at + plan.row_block + group * GROUP_ROWS + t] for t in range(GROUP_ROWS)]

            def col_group(step, total):
                columns = [
                    pl.multiple_of(table[at + plan.col_block + step * GROUP_COLS + q] * SIDE, SIDE)
                    for q in range(GROUP_COLS)
                ]
                tiles = [
                    jnp.concatenate(
                        [root[block_at(block), pl.ds(shift + column, SIDE)] for column in columns], axis=1
                    )
                    for shift in (0, cols)
                    for block in blocks
                ]
                start = pl.multiple_of((base + step * GROUP_COLS) * SIDE, GROUP_COLS * SIDE)
                made = jnp.dot(
                    jnp.concatenate(tiles, axis=0),
                    weights[pl.ds(start, GROUP_COLS * SIDE), :],
                    preferred_element_type=jnp.float32,
                )
                return total + fold_all(made)

            total = lax.fori_loop(
                0, groups, col_group, jnp.zeros((GROUP_ROWS * SIDE, SIDE), jnp.float32)
            )
            for t in range(GROUP_ROWS):
                slot = table[at + plan.row_slot + group * GROUP_ROWS + t]
                value = total[t * SIDE : (t + 1) * SIDE]
                if second:
                    value = value - known[block_at(slot), :]
                else:
                    everything[block_at(slot), :] = value
                for out, other in zip(outs, hops):

                    @pl.when(hop == other)
                    def _(out=out, other=other, slot=slot, value=value):
                        out[block_at(slot - other * capacity), :] = value

            return carry

        return lax.fori_loop(0, (table[at] + GROUP_ROWS - 1) // GROUP_ROWS, row_group, carry)

    lax.fori_loop(0, jobs, per_job, jnp.int32(0))


def root_partials(where, plan, table, root, gathered, hops, owned, capacity, known=None):
    rows, wide = root.shape
    nodes = len(hops) * owned
    room = min(nodes * plan.cols, rounded(gathered.shape[0] // SIDE, GROUP_COLS) + nodes * GROUP_COLS)
    copies = ROOT_COPIES if rows % (ROOT_COPIES * 16) == 0 else 1
    outs = [shape_f32(capacity * SIDE, SIDE)] * len(hops)
    if known is None:
        outs = outs + [shape_f32(len(hops) * capacity * SIDE, SIDE)]
    return call(
        functools.partial(root_body, plan, hops, owned, capacity, known is not None),
        outs,
        [where, table],
        [gathered] if known is None else [gathered, known],
        [
            pltpu.VMEM((room * SIDE, PAIR), jnp.bfloat16),
            pltpu.VMEM((rows, wide), jnp.bfloat16),
            pltpu.SMEM((nodes,), jnp.int32),
            pltpu.SemaphoreType.DMA((copies,)),
        ],
        [root],
    )


def link_body(plan, table, firsts, link, out):
    nodes = link.shape[1] // SIDE

    def per_node(node, carry):
        at = node * plan.stride
        block = beside(link[:, block_at(node)])

        def step(t, carry):
            first = table[at + plan.row_first + t]
            slot = table[at + plan.row_slot + t]
            made = jnp.dot(above(firsts[block_at(first), :]), block, preferred_element_type=jnp.float32)
            out[block_at(slot), :] = fold_all(made)
            return carry

        return lax.fori_loop(0, table[at], step, carry)

    lax.fori_loop(0, nodes, per_node, jnp.int32(0))


def first_body(row_blocks, ranks_col, where_ref, pattern, position, pattern_two, position_two, kids, *refs):
    mine, near, far, packed, *rest = refs
    blocks_two, (off, sums, total) = rest[:ranks_col], rest[ranks_col:]
    row_start = where_ref[0] * row_blocks
    col_index = where_ref[1]
    owned = off.shape[1] // SIDE
    owned_two = pattern_two.shape[1] // ranks_col
    total[...] = mine[...] + near[...] + far[...]
    sums[...] = jnp.zeros(sums.shape, jnp.float32)
    for local in range(owned):
        node = col_index * owned + local
        lanes = slice(local * SIDE, (local + 1) * SIDE)

        def step(block, carry):
            place = row_start + block
            slot = position[place, node]
            active = pattern[place, node] > 0

            @pl.when(active)
            def _():
                value = total[block_at(slot), :]
                off[block_at(block), lanes] = -value
                sums[0:SIDE, lanes] += inner(packed[block_at(slot), :], value)

            @pl.when(jnp.logical_not(active))
            def _():
                off[block_at(block), lanes] = jnp.zeros((SIDE, SIDE), jnp.float32)

            for kid in range(2):
                child = kids[2 * local + kid]
                hop = col_index ^ (child // owned_two)
                slot_two = position_two[place, child]

                @pl.when(pattern_two[place, child] > 0)
                def _(kid=kid, hop=hop, slot_two=slot_two):
                    for other in range(ranks_col):

                        @pl.when(hop == other)
                        def _(other=other):
                            sums[(1 + kid) * SIDE : (2 + kid) * SIDE, lanes] += inner(
                                total[block_at(slot), :], blocks_two[other][block_at(slot_two), :]
                            )

            return carry

        lax.fori_loop(0, row_blocks, step, jnp.int32(0))


def second_body(row_blocks, where_ref, pattern, position, mine, near, far, packed, off, sums, total):
    row_start = where_ref[0] * row_blocks
    col_index = where_ref[1]
    owned = off.shape[1] // SIDE
    total[...] = mine[...] + near[...] + far[...]
    sums[...] = jnp.zeros(sums.shape, jnp.float32)
    for local in range(owned):
        node = col_index * owned + local
        lanes = slice(local * SIDE, (local + 1) * SIDE)

        def step(block, carry):
            place = row_start + block
            slot = position[place, node]
            active = pattern[place, node] > 0

            @pl.when(active)
            def _():
                value = total[block_at(slot), :]
                off[block_at(block), lanes] = -value
                sums[:, lanes] += inner(packed[block_at(slot), :], value)

            @pl.when(jnp.logical_not(active))
            def _():
                off[block_at(block), lanes] = jnp.zeros((SIDE, SIDE), jnp.float32)

            return carry

        lax.fori_loop(0, row_blocks, step, jnp.int32(0))


def tail_body(kids, diag, sums, link, diagonal, made):
    owned = diag.shape[1] // SIDE
    for local in range(owned):
        lanes = slice(local * SIDE, (local + 1) * SIDE)
        own = diag[:, lanes] + sums[0:SIDE, lanes]
        diagonal[:, lanes] = own
        for kid in range(2):
            step = link[:, block_at(kids[2 * local + kid])]
            share = sums[(1 + kid) * SIDE : (2 + kid) * SIDE, lanes]
            across = jnp.dot(own, step, precision=EXACT, preferred_element_type=jnp.float32) - share
            at = (2 * local + kid) * SIDE
            made[at : at + SIDE, 0:SIDE] = -across
            made[at : at + SIDE, SIDE:PAIR] = inner(step, across)


def swap_col(value, hop):
    ranks = lax.axis_size("col")
    return lax.ppermute(value, "col", [(c, c ^ hop) for c in range(ranks)])


def gather_col(value, *before):
    across = after(swap_col(value, 2), *before)
    return [value, swap_col(value, 1), across, swap_col(across, 1)]


def exchange_col(value, col_index, chunk):
    piece = lambda hop: lax.dynamic_slice_in_dim(value, (col_index ^ hop) * chunk, chunk, 0)
    moved = [swap_col(piece(hop), hop) for hop in (3, 2, 1)]
    return jnp.concatenate([piece(0), moved[2], moved[1], moved[0]], axis=0)


def turn(pieces):
    ranks = len(pieces)
    return jnp.concatenate(
        [
            lax.ppermute(
                piece,
                ("row", "col"),
                [(r * ranks + c, (c ^ u) * ranks + r) for r in range(ranks) for c in range(ranks)],
            )
            for u, piece in enumerate(pieces)
        ],
        axis=0,
    )


def scatter_col(parts):
    relay = parts[2] + swap_col(parts[3], 1)
    return parts[0], swap_col(parts[1], 1), swap_col(relay, 2), relay


def sum_row(value):
    ranks = lax.axis_size("row")
    reach = 1
    while reach < ranks:
        value = value + lax.ppermute(value, "row", [(r, r ^ reach) for r in range(ranks)])
        reach *= 2
    return value


def counts(pattern, row_blocks, ranks_col):
    blocks, nodes = pattern.shape
    return jnp.sum(
        pattern.reshape(blocks // row_blocks, row_blocks, ranks_col, nodes // ranks_col), axis=(1, 3)
    )


def positions(pattern, row_blocks, ranks_col):
    blocks, nodes = pattern.shape
    owned = nodes // ranks_col
    many = owned * row_blocks
    flat = (
        pattern.reshape(blocks // row_blocks, row_blocks, ranks_col, owned)
        .transpose(0, 2, 3, 1)
        .reshape(blocks // row_blocks, ranks_col, many)
    )
    before = (jnp.arange(many)[None, :] < jnp.arange(many)[:, None]).astype(jnp.int32)
    rank = jnp.sum(flat[:, :, None, :] * before[None, None], axis=-1)
    return (
        rank.reshape(blocks // row_blocks, ranks_col, owned, row_blocks)
        .transpose(0, 3, 1, 2)
        .reshape(blocks, nodes)
        .astype(jnp.int32)
    )


def after(value, *others):
    return lax.optimization_barrier((value, *others))[0]


def sparse_plan(
    capacities,
    root_inverse,
    lower_one,
    pattern_one,
    diag_one,
    lower_two,
    pattern_two,
    parent_two,
    lower_parent,
    diag_two,
):
    capacity_one, capacity_two, capacity_line = capacities
    rows_here, cols_here = root_inverse.shape
    row_blocks = rows_here // SIDE
    col_blocks = cols_here // SIDE
    ranks_row = lax.axis_size("row")
    ranks_col = lax.axis_size("col")
    turned = ranks_row == ranks_col
    group = ranks_row // ranks_col
    row_index = lax.axis_index("row")
    col_index = lax.axis_index("col")
    owned_one = lower_one.shape[1] // SIDE
    owned_two = lower_two.shape[1] // SIDE
    where = jnp.stack([row_index, col_index]).astype(jnp.int32)

    packed_one = pack(where, pattern_one, lower_one, capacity_one)
    rows_one = lax.all_gather(packed_one, "row", axis=0, tiled=True)
    packed_two = pack(where, pattern_two, after(lower_two, packed_one), capacity_two)

    position_one = positions(pattern_one, row_blocks, ranks_col)
    position_two = positions(pattern_two, row_blocks, ranks_col)
    held_two = counts(pattern_two, row_blocks, ranks_col)
    base_two = jnp.concatenate([jnp.zeros((ranks_row, 1), jnp.int32), jnp.cumsum(held_two, axis=1)], axis=1)
    base_two = base_two.astype(jnp.int32)
    own_rows = lambda value: lax.dynamic_slice_in_dim(value, row_index * row_blocks, row_blocks, 0)
    own_cols = lambda value: lax.dynamic_slice_in_dim(value, col_index * col_blocks, col_blocks, 0)
    hop_one = ((jnp.arange(pattern_one.shape[1]) // owned_one) ^ col_index)[None, :]
    hop_two = ((jnp.arange(pattern_two.shape[1]) // owned_two) ^ col_index)[None, :]
    part = (jnp.arange(col_blocks) // row_blocks)[:, None]
    give_one = hop_one * capacity_one + own_rows(position_one)
    give_two = hop_two * capacity_two + own_rows(position_two)
    take_one = (hop_one * group + part) * capacity_one + own_cols(position_one)
    if turned:
        start_two = lax.dynamic_slice_in_dim(base_two, col_index, 1, 0)[:, :ranks_col]
        take_two = jnp.repeat(start_two, owned_two, axis=1) + own_cols(position_two)
    else:
        take_two = (hop_two * group + part) * capacity_two + own_cols(position_two)
    elder = (parent_two[None, :] == jnp.arange(pattern_one.shape[1])[:, None]).astype(jnp.int32)
    first_two = jnp.sum(give_one[:, :, None] * elder[None], axis=1)
    plan, table_one = make_plan(
        own_rows(pattern_one), give_one, give_one, own_cols(pattern_one), take_one
    )
    _, table_two = make_plan(own_rows(pattern_two), give_two, first_two, own_cols(pattern_two), take_two)

    local_ids = col_index * owned_one + jnp.arange(owned_one, dtype=jnp.int32)
    is_kid = parent_two[None, :] == local_ids[:, None]
    ids = jnp.arange(parent_two.shape[0], dtype=jnp.int32)[None, :]
    first_kid = jnp.min(jnp.where(is_kid, ids, ids.shape[1] - 1), axis=1)
    last_kid = jnp.max(jnp.where(is_kid, ids, 0), axis=1)
    kids = jnp.stack([first_kid, last_kid], axis=1).reshape(2 * owned_one)
    beside_two = gather_col(packed_two, table_one, table_two, kids)
    link = jnp.stack(gather_col(after(lower_parent, packed_two))).reshape(ranks_col, SIDE, owned_two * SIDE)
    link = jnp.concatenate(
        [
            lax.dynamic_index_in_dim(link, col_index ^ owner, 0, keepdims=False)
            for owner in range(ranks_col)
        ],
        axis=1,
    )
    if turned:
        piece_rows = capacity_line * SIDE // (ranks_col * ranks_col)
        own_base = lax.dynamic_slice_in_dim(base_two, row_index, 1, 0)[0]
        pieces = call(
            functools.partial(line_body, ranks_col, piece_rows),
            [shape_f32(piece_rows, SIDE)] * ranks_col,
            [where, own_base],
            beside_two,
            [pltpu.VMEM((capacity_line * SIDE, SIDE), jnp.float32)],
        )
        root = split_root(after(root_inverse, *pieces))
        ahead_two = after(turn(pieces), root)
    else:
        root = split_root(root_inverse)
        ahead_two = packed_two
    rows_two = lax.all_gather(ahead_two, "row", axis=0, tiled=True)
    rows_one = after(rows_one, root, ahead_two)
    gathered_one = exchange_col(rows_one, col_index, group * capacity_one * SIDE)
    *partial_one, every_one = root_partials(
        where, plan, table_one, after(root, link), gathered_one, range(ranks_col), owned_one, capacity_one
    )
    mine_one, near_one, far_one, relay_one = scatter_col(partial_one)
    every_one = after(every_one, relay_one)
    known_two = call(
        functools.partial(link_body, plan),
        shape_f32(ranks_col * capacity_two * SIDE, SIDE),
        [table_two],
        [every_one, link],
    )
    far_one = after(far_one, known_two)
    rows_two = after(rows_two, far_one)
    if turned:
        gathered_two = rows_two
    else:
        gathered_two = exchange_col(rows_two, col_index, group * capacity_two * SIDE)
    partial_two = root_partials(
        where, plan, table_two, root, gathered_two, range(ranks_col), owned_two, capacity_two, known_two
    )
    far_one = after(far_one, *partial_two)
    off_one, inner_one, _ = call(
        functools.partial(first_body, row_blocks, ranks_col),
        [
            shape_f32(rows_here, owned_one * SIDE),
            shape_f32(3 * SIDE, owned_one * SIDE),
            shape_f32(capacity_one * SIDE, SIDE),
        ],
        [where, pattern_one, position_one, pattern_two, position_two, kids],
        [mine_one, near_one, far_one, packed_one, *beside_two],
    )
    relay_two = after(partial_two[2], off_one) + swap_col(partial_two[3], 1)
    sums_two = [partial_two[0], swap_col(partial_two[1], 1), swap_col(relay_two, 2)]
    inner_one = sum_row(inner_one)
    diagonal_first, made = call(
        tail_body,
        [shape_f32(SIDE, owned_one * SIDE), shape_f32(2 * owned_one * SIDE, PAIR)],
        [kids],
        [diag_one, inner_one, link],
    )
    off_two, inner_two, _ = call(
        functools.partial(second_body, row_blocks),
        [
            shape_f32(rows_here, owned_two * SIDE),
            shape_f32(SIDE, owned_two * SIDE),
            shape_f32(capacity_two * SIDE, SIDE),
        ],
        [where, pattern_two, position_two],
        [*sums_two, packed_two],
    )
    made_parts = gather_col(made, inner_two)
    made_all = jnp.concatenate(made_parts, axis=0).reshape(ranks_col, owned_one, 2, SIDE, PAIR)
    chosen = []
    for local in range(owned_two):
        child = col_index * owned_two + local
        parent = lax.dynamic_index_in_dim(parent_two, child, 0, keepdims=False)
        later = jnp.sum(jnp.logical_and(parent_two == parent, ids[0] < child).astype(jnp.int32))
        hop = col_index ^ (parent // owned_one)
        chosen.append(
            lax.dynamic_slice(
                made_all, (hop, parent % owned_one, later, 0, 0), (1, 1, 1, SIDE, PAIR)
            ).reshape(SIDE, PAIR)
        )
    minus_across = jnp.concatenate([c[:, :SIDE] for c in chosen], axis=1)
    known = diag_two + jnp.concatenate([c[:, SIDE:] for c in chosen], axis=1)

    return off_one, diagonal_first, off_two, minus_across, known + sum_row(inner_two)


def ladder(full_one, full_two, ranks_col):
    steps = []
    for one, two, line in ((11, 17, 56), (13, 21, 66), (16, 32, 128)):
        step = (
            rounded(one * full_one, 16) // 16,
            rounded(two * full_two, 32) // 32,
            rounded(line * full_two * ranks_col, 128) // 128,
        )
        if step not in steps:
            steps.append(step)
    return steps


def level_body(steps, row_blocks, ranks_col, one, two, level):
    def held(pattern):
        blocks, nodes = pattern.shape
        ranks_row = blocks // row_blocks
        rows = lax.broadcasted_iota(jnp.int32, (ranks_row, blocks), 0)
        inside = lax.broadcasted_iota(jnp.int32, (ranks_row, blocks), 1) // row_blocks == rows
        cols = lax.broadcasted_iota(jnp.int32, (nodes, ranks_col), 1)
        owner = lax.broadcasted_iota(jnp.int32, (nodes, ranks_col), 0) // (nodes // ranks_col) == cols
        by_row = jnp.dot(
            inside.astype(jnp.float32), pattern[...].astype(jnp.float32), preferred_element_type=jnp.float32
        )
        return jnp.dot(by_row, owner.astype(jnp.float32), preferred_element_type=jnp.float32)

    held_one, held_two = held(one), held(two)
    most = (jnp.max(held_one), jnp.max(held_two), jnp.max(jnp.sum(held_two, axis=1, keepdims=True)))
    found = jnp.int32(0)
    for step in steps[:-1]:
        over = functools.reduce(jnp.logical_or, [m > limit for m, limit in zip(most, step)])
        found = found + over.astype(jnp.int32)
    level[0] = found


def local(root_inverse, lower_one, pattern_one, diag_one, lower_two, pattern_two, *others):
    row_blocks = root_inverse.shape[0] // SIDE
    ranks_col = lax.axis_size("col")
    steps = ladder(
        row_blocks * lower_one.shape[1] // SIDE, row_blocks * lower_two.shape[1] // SIDE, ranks_col
    )
    operands = (root_inverse, lower_one, pattern_one, diag_one, lower_two, pattern_two, *others)
    if len(steps) == 1:
        return sparse_plan(steps[0], *operands)
    level = pl.pallas_call(
        functools.partial(level_body, steps, row_blocks, ranks_col),
        out_shape=jax.ShapeDtypeStruct((1,), jnp.int32),
        in_specs=[VMEM_SPEC, VMEM_SPEC],
        out_specs=SMEM_SPEC,
    )(pattern_one, pattern_two)
    return lax.switch(level[0], [functools.partial(sparse_plan, step) for step in steps], *operands)


def solution(mesh):
    return jax.shard_map(
        local,
        mesh=mesh,
        in_specs=(
            P(("pole", "row"), "col"),
            P(("pole", "row"), "col"),
            P(),
            P("pole", "col"),
            P(("pole", "row"), "col"),
            P(),
            P(),
            P("pole", "col"),
            P("pole", "col"),
        ),
        out_specs=(
            P(("pole", "row"), "col"),
            P("pole", "col"),
            P(("pole", "row"), "col"),
            P("pole", "col"),
            P("pole", "col"),
        ),
        check_vma=False,
    )
```
